128 devices in a mesh: dp: 64 (over x, y, z_hi, core), tensor: 2 (over z_lo).
Axes of the slice: x: 4, y: 4, z: 4 (z_hi: 2, z_lo: 2; z = z_hi * 2 + z_lo), core: 2. Of those that a mesh axis runs over, the one named last changes fastest.
Arguments:
- block_input: bfloat16 [8192, 1024], P('dp'), may hold values from -120 to 120
- cotangent: bfloat16 [8192, 1024], P('dp'), may hold values from -16 to 16
- qkv_weight: bfloat16 [1, 1024, 3072], P(None, None, 'tensor'), may hold values from -2 to 2
- dense_weight: bfloat16 [1, 1024, 1024], P(None, None, 'tensor'), may hold values from -1 to 1
- up_weight: bfloat16 [1, 1024, 4096], P(None, None, 'tensor'), may hold values from -0.1875 to 0.1875
- down_weight: bfloat16 [1, 1024, 4096], P(None, None, 'tensor'), may hold values from -0.09375 to 0.09375
- up_bias: float32 [1, 4096], P(None, 'tensor'), may hold values from -3 to 3
- down_bias: float32 [1, 1024], replicated, may hold values from -3 to 3
- norm_gain: float32 [1, 2, 1024], replicated, may hold values from 0.1 to 1.9
- norm_bias: float32 [1, 2, 1024], replicated, may hold values from -3 to 3
- lengths: int32 [96], replicated, may hold values from 32 to 128, as said below
- owner_group: int32 [96], replicated, may hold values from 0 to 63
- row_offset: int32 [96], replicated, may hold values from 0 to 64
Outputs:
- block_output: float32 [8192, 1024], P('dp')
- input_grad: float32 [8192, 1024], P('dp')
- qkv_grad: float32 [1, 1024, 3072], P(None, 'dp', 'tensor')
- dense_grad: float32 [1, 1024, 1024], P(None, 'dp', 'tensor')
- up_grad: float32 [1, 1024, 4096], P(None, 'dp', 'tensor')
- down_grad: float32 [1, 1024, 4096], P(None, 'dp', 'tensor')
- up_bias_grad: float32 [1, 4, 1024], P(None, 'tensor', 'dp')
- down_bias_grad: float32 [1, 1024], P(None, 'dp')
- norm_gain_grad: float32 [1, 2, 1024], P(None, None, 'dp')
- norm_bias_grad: float32 [1, 2, 1024], P(None, None, 'dp')
The draws below stay inside these ranges and needn't reach their ends.
Inputs may be any that keep to these rules, and one draw needn't show every extreme that they name: Sequence s occupies rows row_offset[s] to row_offset[s] + lengths[s] - 1 of data group owner_group[s]; sequences of one group do not meet, owner_group never falls along s, and every group holds one or two sequences with 64 or more tokens together.
All inputs are finite; a program needn't handle non-finite values.
Results may differ from the reference program's by a relative error of at most 0.0087.
Values sent between devices are 32-bit elements; how exact they have to be, the bound alone decides.
No kernel may reach another device: no remote copies, remote signals or barrier semaphores. Data moves between devices by JAX's collectives and lax.ppermute only.
A program may use at most 128 MiB of HBM per device.

```python
import math
import jax
import jax.numpy as jnp
from jax import lax

D = 1024
HEADS = 16
HEAD_DIM = 64
ROTARY = 16
FF = 4096
LAYERS = 1
TOK_DEV = 128
TOKENS = 8192
N_DP = 64


def sequence_layout(key):
    normal_base = jax.random.fold_in(key, 11)
    pair_count = N_DP // 2
    streams = jax.random.split(normal_base, 6)
    layout_flip = jax.random.randint(streams[0], (pair_count,), 0, 2)
    single = jax.random.randint(streams[1], (pair_count,), TOK_DEV // 2, TOK_DEV + 1)
    full_pair = jax.random.randint(streams[2], (), 0, pair_count)
    pair_index = jnp.arange(pair_count, dtype=jnp.int32)
    single = jnp.where(pair_index == full_pair, TOK_DEV, single)
    first_length = jax.random.randint(streams[3], (pair_count,), TOK_DEV // 4, TOK_DEV // 2 + 1)
    second_length = jax.random.randint(streams[4], (pair_count,), TOK_DEV // 4, TOK_DEV // 2 + 1)
    widest = jax.random.randint(streams[5], (), 0, pair_count)
    first_length = jnp.where(pair_index == widest, TOK_DEV // 2, first_length)
    second_length = jnp.where(pair_index == (widest + 1) % pair_count, TOK_DEV // 4, second_length)
    single_first = layout_flip == 0
    length = jnp.stack([jnp.where(single_first, single, first_length), jnp.where(single_first, first_length, second_length), jnp.where(single_first, second_length, single)], axis=1)
    group_ids = jnp.stack([2 * pair_index, jnp.where(single_first, 2 * pair_index + 1, 2 * pair_index), 2 * pair_index + 1], axis=1)
    offset = jnp.stack([jnp.zeros_like(pair_index), jnp.where(single_first, 0, first_length), jnp.where(single_first, first_length, 0)], axis=1)
    return (length.reshape(-1).astype(jnp.int32), group_ids.reshape(-1).astype(jnp.int32), offset.reshape(-1).astype(jnp.int32))


def draw_lengths(key, part):
    return sequence_layout(key)[0]


def draw_owner_group(key, part):
    return sequence_layout(key)[1]


def draw_row_offset(key, part):
    return sequence_layout(key)[2]


def draw_block_input(key, part):
    values = jnp.clip(jax.random.normal(key, (TOKENS, D), jnp.float32), -4.0, 4.0)
    return values.astype(jnp.bfloat16)


def draw_qkv_weight(key, part):
    normal_base = jnp.clip(jax.random.normal(key, (LAYERS, D, HEADS, 3, HEAD_DIM), jnp.float32), -6.0, 6.0) / math.sqrt(D)
    return normal_base.reshape(LAYERS, D, 3 * D).astype(jnp.bfloat16)


def spiked(array, rng, source, target, parts, factor):
    def block_of(dim):
        return (jnp.arange(array.shape[dim]) // (array.shape[dim] // parts)).reshape((-1,) + (1,) * (array.ndim - 1 - dim))

    near = jax.random.permutation(rng, parts)[block_of(target)]
    second = (block_of(target) + parts // 2) % parts
    return jnp.where((block_of(source) == near) | (block_of(source) == second), factor * array, array)


def levels(own_key, shape, shards, low, top_value):
    def one(dim, parts):
        draws = jax.random.uniform(jax.random.fold_in(jax.random.fold_in(own_key, 6), dim), (parts,), jnp.float32, low / len(shards), top_value / len(shards))
        return jnp.repeat(jnp.exp(draws), shape[dim] // parts).reshape((-1,) + (1,) * (len(shape) - dim - 1))

    loudness = one(*shards[0])
    for cut in shards[1:]:
        loudness = loudness * one(*cut)
    return loudness


def gaussian(rng, extent, deviation, reach, shards=(), kind=jnp.bfloat16):
    factor_of = levels(rng, extent, shards, -0.22, 0.18) if shards else 1.0
    array = jax.random.normal(rng, extent, jnp.float32) * deviation * factor_of
    return jnp.minimum(jnp.maximum(array, -reach), reach).astype(kind)


def bell_draw_with(rng, dims, spread, reach, shards, heavy, held_as=jnp.bfloat16):
    result = spread * jax.random.normal(rng, dims, jnp.float32)
    if shards:
        result = result * levels(rng, dims, shards, -0.22, 0.18)
    return jnp.clip(spiked(result, jax.random.fold_in(rng, 3), *heavy), -reach, reach).astype(held_as)


def setup_inputs(seed: int = 0) -> dict:
    seeds = jax.random.split(jax.random.key(seed), 14)
    block_input = draw_block_input(jax.random.fold_in(seeds[13], 71), 0)
    cotangent = bell_draw_with(seeds[1], (TOKENS, D), 1.0, 16.0, ((0, 64),), (0, 1, 64, 4.0))
    qkv_weight = draw_qkv_weight(jax.random.fold_in(seeds[13], 71), 0)
    dense_weight = gaussian(seeds[3], (LAYERS, D, D), (D // 32) ** -0.5, 1.0, ((2, 2),))
    up_weight = gaussian(seeds[4], (LAYERS, D, FF), D ** -0.5, 0.1875, ((2, 2),))
    down_weight = gaussian(seeds[5], (LAYERS, D, FF), FF ** -0.5, 0.09375, ((2, 2),))
    up_bias = gaussian(seeds[6], (LAYERS, FF), 0.5, 3.0, ((1, 2),), jnp.float32)
    down_bias = gaussian(seeds[7], (LAYERS, D), 0.5, 3.0, (), jnp.float32)
    norm_gain = jnp.clip(1.0 + 0.18 * jax.random.normal(seeds[8], (LAYERS, 2, D), jnp.float32), 0.1, 1.9)
    norm_bias = gaussian(seeds[9], (LAYERS, 2, D), 0.5, 3.0, (), jnp.float32)
    lengths = draw_lengths(jax.random.fold_in(seeds[13], 71), 0)
    owner_group = draw_owner_group(jax.random.fold_in(seeds[13], 71), 0)
    row_offset = draw_row_offset(jax.random.fold_in(seeds[13], 71), 0)
    return dict(block_input=block_input, cotangent=cotangent, qkv_weight=qkv_weight, dense_weight=dense_weight, up_weight=up_weight, down_weight=down_weight, up_bias=up_bias, down_bias=down_bias, norm_gain=norm_gain, norm_bias=norm_bias, lengths=lengths, owner_group=owner_group, row_offset=row_offset)


epsilon = 1e-05

def layout_rows(lengths, owner_group, row_offset, row_index, group_rows):
    first_row = owner_group * group_rows + row_offset
    inside = (row_index[:, None] >= first_row[None, :]) & (row_index[:, None] < (first_row + lengths)[None, :])
    number = jnp.arange(lengths.shape[0], dtype=jnp.int32) + 1
    segment = (lax.optimization_barrier(jnp.sum(jnp.where(inside, number[None, :], 0), axis=1)) - 1).astype(jnp.int32)
    position = lax.optimization_barrier(jnp.sum(jnp.where(inside, row_index[:, None] - first_row[None, :], 0), axis=1)).astype(jnp.int32)
    return (segment, position)

def rotary_tables(position):
    half_rot = ROTARY // 2
    frequency = 1.0 / 10000.0 ** (jnp.arange(half_rot, dtype=jnp.float32) * 2.0 / ROTARY)
    angles = position.astype(jnp.float32)[:, None] * frequency[None, :]
    angles = jnp.concatenate([angles, angles], axis=1)
    return (jnp.cos(angles), jnp.sin(angles))

def rotate(tensor_rows, cosine_table, sine_table):
    rotary_part = tensor_rows[..., :ROTARY]
    first_half = rotary_part[..., :ROTARY // 2]
    second_half = rotary_part[..., ROTARY // 2:]
    turned = jnp.concatenate([-second_half, first_half], axis=-1)
    moved = rotary_part * cosine_table[:, None, :] + turned * sine_table[:, None, :]
    return jnp.concatenate([moved, tensor_rows[..., ROTARY:]], axis=-1)

def rotate_back(grad_rows, cosine_table, sine_table):
    rotary_part = grad_rows[..., :ROTARY]
    scaled = rotary_part * sine_table[:, None, :]
    first_half = scaled[..., :ROTARY // 2]
    second_half = scaled[..., ROTARY // 2:]
    moved = rotary_part * cosine_table[:, None, :] + jnp.concatenate([second_half, -first_half], axis=-1)
    return jnp.concatenate([moved, grad_rows[..., ROTARY:]], axis=-1)

def normalize(hidden, gain_row, bias_row):
    row_mean = lax.optimization_barrier(jnp.mean(hidden, axis=-1, keepdims=True))
    centred = hidden - row_mean
    inv_scale = lax.rsqrt(lax.optimization_barrier(jnp.mean(centred * centred, axis=-1, keepdims=True)) + epsilon)
    unit_rows = centred * inv_scale
    return (unit_rows * gain_row + bias_row, unit_rows, inv_scale)

def normalize_back(grad_rows, unit_rows, inv_scale, gain_row):
    scaled = grad_rows * gain_row
    return inv_scale * (scaled - lax.optimization_barrier(jnp.mean(scaled, axis=-1, keepdims=True)) - unit_rows * lax.optimization_barrier(jnp.mean(scaled * unit_rows, axis=-1, keepdims=True)))

def gelu_exact(values):
    return 0.5 * values * (1.0 + lax.erf(values * 0.7071067811865476))

def gelu_slope(values):
    return 0.5 * (1.0 + lax.erf(values * 0.7071067811865476)) + values * jnp.exp(-0.5 * values * values) * 0.3989422804014327

def allowed_pairs(segment):
    order_rows = jnp.arange(segment.shape[0])
    return (segment[:, None] == segment[None, :]) & (order_rows[None, :] <= order_rows[:, None])

def group_attend(packed):
    queries, key_rows, value_rows, segment = packed
    allowed = allowed_pairs(segment)
    scores = jnp.einsum('qhd,khd->hqk', queries.astype(jnp.float32), key_rows.astype(jnp.float32))
    scores = jnp.where(allowed[None], scores, -1e+30)
    highest = lax.optimization_barrier(jnp.max(scores, axis=-1, keepdims=True))
    weights = jnp.where(allowed[None], jnp.exp(scores - highest), 0.0)
    totals = lax.optimization_barrier(jnp.sum(weights, axis=-1, keepdims=True))
    probs = (weights / totals).astype(jnp.bfloat16)
    context = jnp.einsum('hqk,khd->qhd', probs.astype(jnp.float32), value_rows.astype(jnp.float32)).astype(jnp.bfloat16)
    return (context, (highest + jnp.log(totals))[..., 0])

def group_back(packed):
    queries, key_rows, value_rows, segment, log_total, context, context_grad = packed
    allowed = allowed_pairs(segment)
    scores = jnp.einsum('qhd,khd->hqk', queries.astype(jnp.float32), key_rows.astype(jnp.float32))
    scores = jnp.where(allowed[None], scores, -1e+30)
    probs = jnp.where(allowed[None], jnp.exp(scores - log_total[..., None]), 0.0)
    probs_grad = jnp.einsum('qhd,khd->hqk', context_grad.astype(jnp.float32), value_rows.astype(jnp.float32))
    offset_terms = lax.optimization_barrier(jnp.sum(context_grad.astype(jnp.float32) * context.astype(jnp.float32), axis=-1)).T
    score_grad = (probs * (probs_grad - offset_terms[..., None])).astype(jnp.bfloat16).astype(jnp.float32)
    query_grad = jnp.einsum('hqk,khd->qhd', score_grad, key_rows.astype(jnp.float32))
    key_grad = jnp.einsum('hqk,qhd->khd', score_grad, queries.astype(jnp.float32))
    value_grad = jnp.einsum('hqk,qhd->khd', probs.astype(jnp.bfloat16).astype(jnp.float32), context_grad.astype(jnp.float32))
    return (query_grad, key_grad, value_grad)

def by_group(tensor_rows):
    return tensor_rows.reshape((tensor_rows.shape[0] // TOK_DEV, TOK_DEV) + tensor_rows.shape[1:])

def reference(block_input, cotangent, qkv_weight, dense_weight, up_weight, down_weight, up_bias, down_bias, norm_gain, norm_bias, lengths, owner_group, row_offset):
    row_total = block_input.shape[0]
    row_index = jnp.arange(row_total, dtype=jnp.int32)
    segment, position = layout_rows(lengths, owner_group, row_offset, row_index, TOK_DEV)
    valid_rows = (segment >= 0).astype(jnp.float32)[:, None]
    cosine_table, sine_table = rotary_tables(position)
    hidden = block_input.astype(jnp.float32)
    saved_list = []
    for layer_index in range(LAYERS):
        heads_norm, heads_unit, heads_inv = normalize(hidden, norm_gain[layer_index, 0], norm_bias[layer_index, 0])
        units_norm, units_unit, units_inv = normalize(hidden, norm_gain[layer_index, 1], norm_bias[layer_index, 1])
        heads_in = heads_norm.astype(jnp.bfloat16)
        units_in = units_norm.astype(jnp.bfloat16)
        projected = jnp.dot(heads_in, qkv_weight[layer_index], preferred_element_type=jnp.float32).reshape(row_total, HEADS, 3, HEAD_DIM)
        hidden_pre = jnp.dot(units_in, up_weight[layer_index], preferred_element_type=jnp.float32) + up_bias[layer_index]
        queries = (rotate(projected[:, :, 0], cosine_table, sine_table) * HEAD_DIM ** (-0.5)).astype(jnp.bfloat16)
        key_rows = rotate(projected[:, :, 1], cosine_table, sine_table).astype(jnp.bfloat16)
        value_rows = projected[:, :, 2].astype(jnp.bfloat16)
        context, log_total = lax.map(group_attend, (by_group(queries), by_group(key_rows), by_group(value_rows), by_group(segment)))
        context = context.reshape(row_total, D)
        activated = gelu_exact(hidden_pre).astype(jnp.bfloat16)
        branch = jnp.dot(context, dense_weight[layer_index].T, preferred_element_type=jnp.float32) + jnp.dot(activated, down_weight[layer_index].T, preferred_element_type=jnp.float32)
        saved_list.append((heads_in, units_in, heads_unit, heads_inv, units_unit, units_inv, queries, key_rows, value_rows, context, log_total, hidden_pre, activated))
        hidden = hidden + valid_rows * (branch + down_bias[layer_index])
    block_output = hidden
    grad_rows = cotangent.astype(jnp.float32)
    results = [None] * LAYERS
    for layer_index in reversed(range(LAYERS)):
        heads_in, units_in, heads_unit, heads_inv, units_unit, units_inv, queries, key_rows, value_rows, context, log_total, hidden_pre, activated = saved_list[layer_index]
        branch_grad = grad_rows * valid_rows
        branch_in = branch_grad.astype(jnp.bfloat16)
        down_bias_grad = lax.optimization_barrier(jnp.sum(branch_grad, axis=0))
        dense_grad = jnp.dot(branch_in.T, context, preferred_element_type=jnp.float32)
        down_grad = jnp.dot(branch_in.T, activated, preferred_element_type=jnp.float32)
        context_grad = jnp.dot(branch_in, dense_weight[layer_index], preferred_element_type=jnp.float32).astype(jnp.bfloat16)
        pre_grad = jnp.dot(branch_in, down_weight[layer_index], preferred_element_type=jnp.float32) * gelu_slope(hidden_pre)
        up_bias_grad = lax.optimization_barrier(jnp.sum(pre_grad, axis=0))
        pre_in = pre_grad.astype(jnp.bfloat16)
        up_grad = jnp.dot(units_in.T, pre_in, preferred_element_type=jnp.float32)
        units_grad = jnp.dot(pre_in, up_weight[layer_index].T, preferred_element_type=jnp.float32)
        query_grad, key_grad, value_grad = lax.map(group_back, (by_group(queries), by_group(key_rows), by_group(value_rows), by_group(segment), log_total, by_group(context.reshape(row_total, HEADS, HEAD_DIM)), by_group(context_grad.reshape(row_total, HEADS, HEAD_DIM))))
        query_grad = rotate_back(query_grad.reshape(row_total, HEADS, HEAD_DIM) * HEAD_DIM ** (-0.5), cosine_table, sine_table)
        key_grad = rotate_back(key_grad.reshape(row_total, HEADS, HEAD_DIM), cosine_table, sine_table)
        value_grad = value_grad.reshape(row_total, HEADS, HEAD_DIM)
        projected_grad = jnp.stack([query_grad, key_grad, value_grad], axis=2).reshape(row_total, 3 * D).astype(jnp.bfloat16)
        qkv_grad = jnp.dot(heads_in.T, projected_grad, preferred_element_type=jnp.float32)
        heads_grad = jnp.dot(projected_grad, qkv_weight[layer_index].T, preferred_element_type=jnp.float32)
        gain_grad = jnp.stack([lax.optimization_barrier(jnp.sum(heads_grad * heads_unit, axis=0)), lax.optimization_barrier(jnp.sum(units_grad * units_unit, axis=0))])
        bias_grad = jnp.stack([lax.optimization_barrier(jnp.sum(heads_grad, axis=0)), lax.optimization_barrier(jnp.sum(units_grad, axis=0))])
        grad_rows = grad_rows + normalize_back(heads_grad, heads_unit, heads_inv, norm_gain[layer_index, 0]) + normalize_back(units_grad, units_unit, units_inv, norm_gain[layer_index, 1])
        results[layer_index] = (qkv_grad, dense_grad, up_grad, down_grad, up_bias_grad.reshape(FF // D, D), down_bias_grad, gain_grad, bias_grad)
    stacked = [jnp.stack([results[layer_index][member] for layer_index in range(LAYERS)]) for member in range(8)]
    return (block_output, grad_rows, stacked[0], stacked[1], stacked[2], stacked[3], stacked[4], stacked[5], stacked[6], stacked[7])
```

```python
import jax
import jax.numpy as jnp
from jax import lax
from jax.sharding import Mesh
from jax.sharding import PartitionSpec as P

HEAD_DIM = 64
ROTARY = 16
DP = ("dp_0", "dp_1", "dp_2", "dp_3")
X, Y, ZH, CORE = DP
TENSOR = "tensor"

epsilon = 1e-05

CONTRACT_COLS = (((1,), (1,)), ((), ()))


def shift(array, axis, step):
    size = lax.axis_size(axis)
    return lax.ppermute(array, axis, [(i, (i + step) % size) for i in range(size)])


def layout_rows(lengths, owner_group, row_offset, row_index, group_rows):
    first_row = owner_group * group_rows + row_offset
    inside = (row_index[:, None] >= first_row[None, :]) & (
        row_index[:, None] < (first_row + lengths)[None, :]
    )
    number = jnp.arange(lengths.shape[0], dtype=jnp.int32) + 1
    segment = jnp.sum(jnp.where(inside, number[None, :], 0), axis=1) - 1
    position = jnp.sum(jnp.where(inside, row_index[:, None] - first_row[None, :], 0), axis=1)
    return (segment, position)


def rotary_tables(position):
    half_rot = ROTARY // 2
    frequency = 1.0 / 10000.0 ** (jnp.arange(half_rot, dtype=jnp.float32) * 2.0 / ROTARY)
    angles = position.astype(jnp.float32)[:, None] * frequency[None, :]
    angles = jnp.concatenate([angles, angles], axis=1)
    return (jnp.cos(angles), jnp.sin(angles))


def rotate(tensor_rows, cosine_table, sine_table):
    rotary_part = tensor_rows[..., :ROTARY]
    first_half = rotary_part[..., : ROTARY // 2]
    second_half = rotary_part[..., ROTARY // 2 :]
    turned = jnp.concatenate([-second_half, first_half], axis=-1)
    moved = rotary_part * cosine_table[:, None, :] + turned * sine_table[:, None, :]
    return jnp.concatenate([moved, tensor_rows[..., ROTARY:]], axis=-1)


def rotate_back(grad_rows, cosine_table, sine_table):
    rotary_part = grad_rows[..., :ROTARY]
    scaled = rotary_part * sine_table[:, None, :]
    first_half = scaled[..., : ROTARY // 2]
    second_half = scaled[..., ROTARY // 2 :]
    moved = rotary_part * cosine_table[:, None, :] + jnp.concatenate(
        [second_half, -first_half], axis=-1
    )
    return jnp.concatenate([moved, grad_rows[..., ROTARY:]], axis=-1)


def unit(hidden):
    row_mean = jnp.mean(hidden, axis=-1, keepdims=True)
    centred = hidden - row_mean
    inv_scale = lax.rsqrt(jnp.mean(centred * centred, axis=-1, keepdims=True) + epsilon)
    return (centred * inv_scale, inv_scale)


def normalize_back(grad_rows, unit_rows, inv_scale, gain_row):
    scaled = grad_rows * gain_row
    return inv_scale * (
        scaled
        - jnp.mean(scaled, axis=-1, keepdims=True)
        - unit_rows * jnp.mean(scaled * unit_rows, axis=-1, keepdims=True)
    )


def gelu_exact(values):
    return 0.5 * values * (1.0 + lax.erf(values * 0.7071067811865476))


def gelu_slope(values):
    return (
        0.5 * (1.0 + lax.erf(values * 0.7071067811865476))
        + values * jnp.exp(-0.5 * values * values) * 0.3989422804014327
    )


def attend(queries, key_rows, value_rows, allowed):
    scores = jnp.einsum("qhd,khd->hqk", queries, key_rows, preferred_element_type=jnp.float32)
    scores = jnp.where(allowed[None], scores, -1e30)
    highest = jnp.max(scores, axis=-1, keepdims=True)
    weights = jnp.where(allowed[None], jnp.exp(scores - highest), 0.0)
    totals = jnp.sum(weights, axis=-1, keepdims=True)
    probs = (weights / totals).astype(jnp.bfloat16)
    context = jnp.einsum(
        "hqk,khd->qhd", probs, value_rows, preferred_element_type=jnp.float32
    ).astype(jnp.bfloat16)
    return (context, (highest + jnp.log(totals))[..., 0])


def attend_back(queries, key_rows, value_rows, allowed, log_total, context, context_grad):
    scores = jnp.einsum("qhd,khd->hqk", queries, key_rows, preferred_element_type=jnp.float32)
    scores = jnp.where(allowed[None], scores, -1e30)
    probs = jnp.where(allowed[None], jnp.exp(scores - log_total[..., None]), 0.0)
    probs_grad = jnp.einsum(
        "qhd,khd->hqk", context_grad, value_rows, preferred_element_type=jnp.float32
    )
    offset_terms = jnp.sum(
        context_grad.astype(jnp.float32) * context.astype(jnp.float32), axis=-1
    ).T
    score_grad = (probs * (probs_grad - offset_terms[..., None])).astype(jnp.bfloat16)
    query_grad = jnp.einsum(
        "hqk,khd->qhd", score_grad, key_rows, preferred_element_type=jnp.float32
    )
    key_grad = jnp.einsum("hqk,qhd->khd", score_grad, queries, preferred_element_type=jnp.float32)
    value_grad = jnp.einsum(
        "hqk,qhd->khd", probs.astype(jnp.bfloat16), context_grad, preferred_element_type=jnp.float32
    )
    return (query_grad, key_grad, value_grad)


def selection(width):
    ix, iy, core = lax.axis_index(X), lax.axis_index(Y), lax.axis_index(CORE)
    row = jnp.arange(width, dtype=jnp.int32)
    half = width // 2
    block = width // 64
    inner = row % block
    zh = (row // block) % 2
    minor = (row // (2 * block)) % 4
    major = (row % half) // (8 * block)
    x_first = row < half
    at_x = jnp.where(x_first, (ix + major + 1) % 4, minor)
    at_y = jnp.where(x_first, minor, (iy + major + 1) % 4)
    feature = (((at_x * 4 + at_y) * 2 + zh) * 2 + core) * block + inner
    column = jnp.arange(width, dtype=jnp.int32)
    return (feature[:, None] == column[None, :]).astype(jnp.bfloat16)


def pick(chosen, rows):
    return lax.dot_general(
        chosen, rows, CONTRACT_COLS, preferred_element_type=jnp.float32
    ).astype(jnp.bfloat16)


def ring_sum(left, right, axis):
    quarter = left.shape[0] // 4
    half = quarter // 2

    def part(start, stop):
        return jnp.dot(left[start:stop], right, preferred_element_type=jnp.float32)

    from_minus = shift(part(half, 3 * half), axis, 1)
    from_plus = shift(part(3 * half, 5 * half), axis, -1)
    low = shift(part(0, half) + from_minus[half:], axis, 1)
    high = shift(part(5 * half, 6 * half) + from_plus[:half], axis, -1)
    own = part(6 * half, 8 * half)
    return (
        own
        + jnp.concatenate([from_plus[half:], from_minus[:half]], axis=0)
        + jnp.concatenate([low, high], axis=0)
    )


def spread_sum(rows, axes):
    count = 1
    for axis in axes:
        count *= lax.axis_size(axis)
    parts = rows.reshape(count, rows.shape[0] // count, rows.shape[1])
    parts = lax.all_to_all(parts, axes, split_axis=0, concat_axis=0, tiled=True)
    return parts.sum(axis=0)


def shards(
    block_input,
    cotangent,
    qkv_weight,
    dense_weight,
    up_weight,
    down_weight,
    up_bias,
    down_bias,
    norm_gain,
    norm_bias,
    lengths,
    owner_group,
    row_offset,
):
    row_count, model_width = block_input.shape
    qkv_weight, dense_weight = qkv_weight[0], dense_weight[0]
    up_weight, down_weight = up_weight[0], down_weight[0]
    norm_gain, norm_bias = norm_gain[0], norm_bias[0]
    qkv_cols = qkv_weight.shape[1]
    head_cols = dense_weight.shape[1]
    hidden_cols = up_weight.shape[1]
    local_heads = head_cols // HEAD_DIM
    table_rows = hidden_cols // model_width

    group = lax.axis_index(DP)
    hidden = block_input.astype(jnp.float32)
    grad_rows = cotangent.astype(jnp.float32)
    near_hidden, near_grad = lax.optimization_barrier(
        (shift(hidden, CORE, 1), shift(grad_rows, CORE, 1))
    )
    own_index = group * row_count + jnp.arange(row_count, dtype=jnp.int32)
    near_index = (group ^ 1) * row_count + jnp.arange(row_count, dtype=jnp.int32)
    segment, position = layout_rows(lengths, owner_group, row_offset, own_index, row_count)
    near_segment, _ = layout_rows(lengths, owner_group, row_offset, near_index, row_count)
    valid_rows = (segment >= 0).astype(jnp.float32)[:, None]
    near_valid = (near_segment >= 0).astype(jnp.float32)[:, None]
    cosine_table, sine_table = rotary_tables(position)
    order_rows = jnp.arange(row_count)
    allowed = (segment[:, None] == segment[None, :]) & (order_rows[None, :] <= order_rows[:, None])

    unit_rows, inv_scale = unit(hidden)
    heads_in = (unit_rows * norm_gain[0] + norm_bias[0]).astype(jnp.bfloat16)
    units_in = (unit_rows * norm_gain[1] + norm_bias[1]).astype(jnp.bfloat16)
    branch_grad = grad_rows * valid_rows
    branch_in = branch_grad.astype(jnp.bfloat16)

    near_unit, _ = unit(near_hidden)
    near_heads_in = (near_unit * norm_gain[0] + norm_bias[0]).astype(jnp.bfloat16)
    near_units_in = (near_unit * norm_gain[1] + norm_bias[1]).astype(jnp.bfloat16)
    near_branch_in = (near_grad * near_valid).astype(jnp.bfloat16)

    chosen = selection(model_width)
    half = model_width // 2
    branch_left = pick(chosen, jnp.concatenate([branch_in, near_branch_in], axis=0))
    units_left = pick(chosen, jnp.concatenate([units_in, near_units_in], axis=0))
    heads_left = pick(chosen, jnp.concatenate([heads_in, near_heads_in], axis=0))

    def both(rows):
        near = lax.optimization_barrier(shift(rows, CORE, 1)) * near_valid
        return jnp.concatenate([rows.astype(jnp.bfloat16), near.astype(jnp.bfloat16)], axis=0)

    hidden_pre = jnp.dot(units_in, up_weight, preferred_element_type=jnp.float32) + up_bias
    activated_wide = gelu_exact(hidden_pre)
    activated = activated_wide.astype(jnp.bfloat16)
    down_right = both(activated_wide)
    column = hidden_cols // 2
    down_x = ring_sum(branch_left[:half], down_right[:, :column], X)
    down_y = ring_sum(branch_left[half:], down_right[:, column:], Y)

    pre_grad = jnp.dot(branch_in, down_weight, preferred_element_type=jnp.float32) * gelu_slope(
        hidden_pre
    )
    pre_in = pre_grad.astype(jnp.bfloat16)
    up_right = both(pre_grad)
    up_x = ring_sum(units_left[:half], up_right[:, :column], X)
    up_y = ring_sum(units_left[half:], up_right[:, column:], Y)

    projected = jnp.dot(heads_in, qkv_weight, preferred_element_type=jnp.float32)
    projected = projected.reshape(row_count, local_heads, 3, HEAD_DIM)
    queries = (rotate(projected[:, :, 0], cosine_table, sine_table) * HEAD_DIM ** (-0.5)).astype(
        jnp.bfloat16
    )
    key_rows = rotate(projected[:, :, 1], cosine_table, sine_table).astype(jnp.bfloat16)
    value_rows = projected[:, :, 2].astype(jnp.bfloat16)
    context, log_total = attend(queries, key_rows, value_rows, allowed)
    context_flat = context.reshape(row_count, head_cols)
    context_right = both(context_flat.astype(jnp.float32))
    partial_rows = lax.dot_general(
        context_flat, dense_weight, CONTRACT_COLS, preferred_element_type=jnp.float32
    ) + lax.dot_general(
        activated, down_weight, CONTRACT_COLS, preferred_element_type=jnp.float32
    )
    branch = partial_rows + shift(partial_rows, TENSOR, 1)
    output = hidden + valid_rows * (branch + down_bias)

    context_grad = (
        jnp.dot(branch_in, dense_weight, preferred_element_type=jnp.float32)
        .astype(jnp.bfloat16)
        .reshape(row_count, local_heads, HEAD_DIM)
    )
    query_grad, key_grad, value_grad = attend_back(
        queries, key_rows, value_rows, allowed, log_total, context, context_grad
    )
    query_grad = rotate_back(query_grad * HEAD_DIM ** (-0.5), cosine_table, sine_table)
    key_grad = rotate_back(key_grad, cosine_table, sine_table)
    projected_wide = jnp.stack([query_grad, key_grad, value_grad], axis=2).reshape(
        row_count, qkv_cols
    )
    projected_grad = projected_wide.astype(jnp.bfloat16)
    qkv_right = both(projected_wide)
    first = (qkv_cols + head_cols) // 2 - head_cols
    none_a = jnp.zeros((2 * row_count, first), jnp.bfloat16)
    none_b = jnp.zeros((2 * row_count, head_cols), jnp.bfloat16)
    mixed_right = jnp.concatenate(
        [
            jnp.concatenate([context_right, none_a], axis=1),
            jnp.concatenate([none_b, qkv_right[:, :first]], axis=1),
        ],
        axis=0,
    )
    mixed_left = jnp.concatenate([branch_left[:half], heads_left[:half]], axis=1)
    qkv_x = ring_sum(mixed_left, mixed_right, X)
    qkv_y = ring_sum(heads_left[half:], qkv_right[:, first:], Y)

    heads_grad = lax.dot_general(
        projected_grad, qkv_weight, CONTRACT_COLS, preferred_element_type=jnp.float32
    )
    units_grad = lax.dot_general(
        pre_in, up_weight, CONTRACT_COLS, preferred_element_type=jnp.float32
    )
    local_back = normalize_back(
        heads_grad, unit_rows, inv_scale, norm_gain[0]
    ) + normalize_back(units_grad, unit_rows, inv_scale, norm_gain[1])
    input_grad = grad_rows + (local_back + shift(local_back, TENSOR, 1))

    small = jnp.concatenate(
        [
            jnp.sum(heads_grad * unit_rows, axis=0)[None],
            jnp.sum(units_grad * unit_rows, axis=0)[None],
            jnp.sum(heads_grad, axis=0)[None],
            jnp.sum(units_grad, axis=0)[None],
            jnp.sum(branch_grad, axis=0)[None],
            jnp.sum(pre_grad, axis=0).reshape(table_rows, model_width),
        ],
        axis=0,
    )
    groups = lax.axis_size(DP)
    block = model_width // groups
    small_rows = small.shape[0]
    small = small.reshape(small_rows, groups, block).swapaxes(0, 1).reshape(groups, -1)
    small = jnp.pad(small, ((0, 0), (0, 128 - small.shape[1])))
    small = lax.all_to_all(small, DP, split_axis=0, concat_axis=0, tiled=True).sum(axis=0)
    norms = small[: 4 * block]
    norms = (norms + shift(small, TENSOR, 1)[: 4 * block]).reshape(4, block)
    small = small[: small_rows * block].reshape(small_rows, block)

    early_x = spread_sum(jnp.concatenate([down_x, up_x], axis=1), (Y, ZH))
    early_y = spread_sum(jnp.concatenate([down_y, up_y], axis=1), (X, ZH))
    late_x = spread_sum(qkv_x, (Y, ZH))
    late_y = spread_sum(qkv_y, (X, ZH))

    qkv_grad = jnp.concatenate([late_x[:, head_cols:], late_y], axis=1)
    dense_grad = late_x[:, :head_cols]
    down_grad = jnp.concatenate([early_x[:, :column], early_y[:, :column]], axis=1)
    up_grad = jnp.concatenate([early_x[:, column:], early_y[:, column:]], axis=1)
    return (
        output,
        input_grad,
        qkv_grad[None],
        dense_grad[None],
        up_grad[None],
        down_grad[None],
        small[5:][None],
        small[4][None],
        norms[:2][None],
        norms[2:][None],
    )


def solution(mesh):
    split = Mesh(
        mesh.devices.reshape(4, 4, 2, 2, mesh.shape["tensor"]),
        (*DP, TENSOR),
    )
    in_specs = (
        P(DP, None),
        P(DP, None),
        P(None, None, "tensor"),
        P(None, None, "tensor"),
        P(None, None, "tensor"),
        P(None, None, "tensor"),
        P(None, "tensor"),
        P(),
        P(),
        P(),
        P(),
        P(),
        P(),
    )
    out_specs = (
        P(DP, None),
        P(DP, None),
        P(None, DP, "tensor"),
        P(None, DP, "tensor"),
        P(None, DP, "tensor"),
        P(None, DP, "tensor"),
        P(None, "tensor", DP),
        P(None, DP),
        P(None, None, DP),
        P(None, None, DP),
    )
    return jax.shard_map(
        shards, mesh=split, in_specs=in_specs, out_specs=out_specs, check_vma=False
    )
```

```python
import functools

import jax
import jax.numpy as jnp
from jax import lax
from jax.experimental import pallas as pl
from jax.experimental.pallas import tpu as pltpu
from jax.sharding import Mesh
from jax.sharding import PartitionSpec as P

HEAD_DIM = 64
ROTARY = 16
DP = ("dp_0", "dp_1", "dp_2", "dp_3")
X, Y, ZH, CORE = DP
TENSOR = "tensor"

epsilon = 1e-05

CONTRACT_COLS = (((1,), (1,)), ((), ()))


def shift(array, axis, step):
    size = lax.axis_size(axis)
    return lax.ppermute(array, axis, [(i, (i + step) % size) for i in range(size)])


def layout_rows(lengths, owner_group, row_offset, row_index, group_rows):
    first_row = owner_group * group_rows + row_offset
    inside = (row_index[:, None] >= first_row[None, :]) & (
        row_index[:, None] < (first_row + lengths)[None, :]
    )
    number = jnp.arange(lengths.shape[0], dtype=jnp.int32) + 1
    segment = jnp.sum(jnp.where(inside, number[None, :], 0), axis=1) - 1
    position = jnp.sum(jnp.where(inside, row_index[:, None] - first_row[None, :], 0), axis=1)
    return (segment, position)


def rotary_tables(position):
    lane = jnp.arange(2 * HEAD_DIM, dtype=jnp.int32) % HEAD_DIM
    half_rot = ROTARY // 2
    frequency = 1.0 / 10000.0 ** ((lane % half_rot).astype(jnp.float32) * 2.0 / ROTARY)
    angles = position.astype(jnp.float32)[:, None] * frequency[None, :]
    turned = (lane < ROTARY)[None, :]
    sign = jnp.where(lane < half_rot, -1.0, 1.0)[None, :]
    return (jnp.where(turned, jnp.cos(angles), 1.0), jnp.where(turned, jnp.sin(angles) * sign, 0.0))


def unit(hidden):
    row_mean = jnp.mean(hidden, axis=-1, keepdims=True)
    centred = hidden - row_mean
    inv_scale = lax.rsqrt(jnp.mean(centred * centred, axis=-1, keepdims=True) + epsilon)
    return (centred * inv_scale, inv_scale)


def normalize_back(grad_rows, unit_rows, inv_scale, gain_row):
    scaled = grad_rows * gain_row
    return inv_scale * (
        scaled
        - jnp.mean(scaled, axis=-1, keepdims=True)
        - unit_rows * jnp.mean(scaled * unit_rows, axis=-1, keepdims=True)
    )


def gelu_exact(values):
    return 0.5 * values * (1.0 + lax.erf(values * 0.7071067811865476))


def gelu_slope(values):
    return (
        0.5 * (1.0 + lax.erf(values * 0.7071067811865476))
        + values * jnp.exp(-0.5 * values * values) * 0.3989422804014327
    )


def attention_kernel(
    projected, context_grad, segment_column, segment_row, cosine, sine, context, grad_wide, grad, turned, raw
):
    rows, cols = projected.shape
    heads = cols // (3 * HEAD_DIM)
    lane = lax.broadcasted_iota(jnp.int32, (rows, 128), 1)
    entry = lane % HEAD_DIM
    scale = HEAD_DIM ** (-0.5)
    tables = []
    for kind in range(3):
        halves = [(2 * kind + side) % 3 for side in range(2)]
        cos_t, sin_t = cosine[...], sine[...]
        low = lane < HEAD_DIM
        for side, what in enumerate(halves):
            here = low if side == 0 else jnp.logical_not(low)
            if what == 0:
                cos_t = jnp.where(here, cos_t * scale, cos_t)
                sin_t = jnp.where(here, sin_t * scale, sin_t)
            if what == 2:
                cos_t = jnp.where(here, 1.0, cos_t)
                sin_t = jnp.where(here, 0.0, sin_t)
        tables.append((cos_t, sin_t))

    def swapped(part):
        up = pltpu.roll(part, 128 - ROTARY // 2, 1)
        down = pltpu.roll(part, ROTARY // 2, 1)
        return jnp.where(entry < ROTARY // 2, up, down)

    for chunk in range(cols // 128):
        at = slice(128 * chunk, 128 * (chunk + 1))
        part = projected[:, at]
        cos_t, sin_t = tables[chunk % 3]
        turned[:, at] = (part * cos_t + swapped(part) * sin_t).astype(jnp.bfloat16)

    allowed = (segment_column[...] == segment_row[...]) & (
        lax.broadcasted_iota(jnp.int32, (rows, rows), 1)
        <= lax.broadcasted_iota(jnp.int32, (rows, rows), 0)
    )

    def product(left, right, dims):
        return lax.dot_general(left, right, (dims, ((), ())), preferred_element_type=jnp.float32)

    for head in range(heads):
        base = 3 * HEAD_DIM * head
        query = turned[:, base : base + HEAD_DIM]
        key = turned[:, base + HEAD_DIM : base + 2 * HEAD_DIM]
        value = turned[:, base + 2 * HEAD_DIM : base + 3 * HEAD_DIM]
        at = slice(HEAD_DIM * head, HEAD_DIM * (head + 1))
        out_grad = context_grad[:, at].astype(jnp.bfloat16)
        scores = jnp.where(allowed, product(query, key, ((1,), (1,))), -1e30)
        highest = jnp.max(scores, axis=-1, keepdims=True)
        weights = jnp.where(allowed, jnp.exp(scores - highest), 0.0)
        probs = weights / jnp.sum(weights, axis=-1, keepdims=True)
        probs_low = probs.astype(jnp.bfloat16)
        out = product(probs_low, value, ((1,), (0,))).astype(jnp.bfloat16)
        context[:, at] = out
        offset = jnp.sum(
            out_grad.astype(jnp.float32) * out.astype(jnp.float32), axis=-1, keepdims=True
        )
        probs_grad = product(out_grad, value, ((1,), (1,)))
        score_grad = (probs * (probs_grad - offset)).astype(jnp.bfloat16)
        raw[:, base : base + HEAD_DIM] = product(score_grad, key, ((1,), (0,)))
        raw[:, base + HEAD_DIM : base + 2 * HEAD_DIM] = product(score_grad, query, ((0,), (0,)))
        raw[:, base + 2 * HEAD_DIM : base + 3 * HEAD_DIM] = product(
            probs_low, out_grad, ((0,), (0,))
        )

    for chunk in range(cols // 128):
        at = slice(128 * chunk, 128 * (chunk + 1))
        part = raw[:, at]
        cos_t, sin_t = tables[chunk % 3]
        back = part * cos_t - swapped(part) * sin_t
        grad_wide[:, at] = back
        grad[:, at] = back.astype(jnp.bfloat16)


def attention(projected, context_grad, segment, cosine, sine):
    rows, cols = projected.shape
    return pl.pallas_call(
        attention_kernel,
        out_shape=(
            jax.ShapeDtypeStruct(context_grad.shape, jnp.bfloat16),
            jax.ShapeDtypeStruct((rows, cols), jnp.float32),
            jax.ShapeDtypeStruct((rows, cols), jnp.bfloat16),
        ),
        scratch_shapes=[
            pltpu.VMEM((rows, cols), jnp.bfloat16),
            pltpu.VMEM((rows, cols), jnp.float32),
        ],
        name="attention",
    )(projected, context_grad, segment[:, None], segment[None, :], cosine, sine)


def product_kernel(count, *refs):
    ins, (to_next, to_last, rest) = refs[: 3 * count], refs[3 * count :]
    column = 0
    for i in range(count):
        left, own, near = ins[3 * i : 3 * i + 3]
        right = jnp.concatenate([own[...], near[...].astype(jnp.bfloat16)], axis=0)
        cols = slice(column, column + own.shape[1])
        column += own.shape[1]
        eighth = left.shape[0] // 8
        targets = (
            (rest, 0), (to_next, 0), (to_next, 1), (to_last, 0), (to_last, 1), (rest, 1), (rest, 2), (rest, 3),
        )
        for block, (out, place) in enumerate(targets):
            out[place * eighth : (place + 1) * eighth, cols] = jnp.dot(
                left[block * eighth : (block + 1) * eighth, :],
                right,
                preferred_element_type=jnp.float32,
            )


def products(*groups):
    rows = groups[0][0].shape[0]
    cols = sum(own.shape[1] for _, own, _ in groups)
    sizes = (rows // 4, rows // 4, rows // 2)
    return pl.pallas_call(
        functools.partial(product_kernel, len(groups)),
        out_shape=tuple(jax.ShapeDtypeStruct((size, cols), jnp.float32) for size in sizes),
        name="products",
    )(*(array for group in groups for array in group))


def moves():
    def along(first, step):
        pairs = []
        for index in range(64):
            x, y, rest, core = index // 16, index // 4 % 4, index % 4, index % 2
            if (core == 0) == first:
                x = (x + step) % 4
            else:
                y = (y + step) % 4
            pairs.append((index, x * 16 + y * 4 + rest))
        return pairs

    return {(first, step): along(first, step) for first in (True, False) for step in (1, -1)}


MOVES = moves()


def ring(array, first, step):
    return lax.ppermute(array, DP, MOVES[first, step])


def tie(values, *others):
    return lax.optimization_barrier((values, *others))[0]


def selection(width):
    ix, iy, iz, core = (lax.axis_index(axis) for axis in DP)
    row = jnp.arange(width, dtype=jnp.int32)
    block = width // 64
    inner = row % block
    at_core = core ^ (1 - row // block % 2)
    at_z = iz ^ (1 - row // (2 * block) % 2)
    second = row // (4 * block) % 4 + 1
    first = row // (16 * block) + 1
    at_x = (ix + jnp.where(core == 0, first, second)) % 4
    at_y = (iy + jnp.where(core == 0, second, first)) % 4
    feature = (((at_x * 4 + at_y) * 2 + at_z) * 2 + at_core) * block + inner
    column = jnp.arange(width, dtype=jnp.int32)
    return (feature[:, None] == column[None, :]).astype(jnp.bfloat16)


def pick(chosen, rows):
    return lax.dot_general(
        chosen, rows, CONTRACT_COLS, preferred_element_type=jnp.float32
    ).astype(jnp.bfloat16)


def shards(
    block_input,
    cotangent,
    qkv_weight,
    dense_weight,
    up_weight,
    down_weight,
    up_bias,
    down_bias,
    norm_gain,
    norm_bias,
    lengths,
    owner_group,
    row_offset,
):
    row_count, model_width = block_input.shape
    qkv_weight, dense_weight = qkv_weight[0], dense_weight[0]
    up_weight, down_weight = up_weight[0], down_weight[0]
    norm_gain, norm_bias = norm_gain[0], norm_bias[0]
    hidden_cols = up_weight.shape[1]
    table_rows = hidden_cols // model_width

    group = lax.axis_index(DP)
    core = lax.axis_index(CORE)
    hidden = block_input.astype(jnp.float32)
    grad_rows = cotangent.astype(jnp.float32)
    near_hidden = shift(hidden, CORE, 1)
    near_grad = shift(grad_rows, CORE, 1)
    own_index = group * row_count + jnp.arange(row_count, dtype=jnp.int32)
    near_index = (group ^ 1) * row_count + jnp.arange(row_count, dtype=jnp.int32)
    segment, position = layout_rows(lengths, owner_group, row_offset, own_index, row_count)
    near_segment, _ = layout_rows(lengths, owner_group, row_offset, near_index, row_count)
    valid_rows = (segment >= 0).astype(jnp.float32)[:, None]
    near_valid = (near_segment >= 0).astype(jnp.float32)[:, None]
    cosine_table, sine_table = rotary_tables(position)

    unit_rows, inv_scale = unit(hidden)
    heads_in = (unit_rows * norm_gain[0] + norm_bias[0]).astype(jnp.bfloat16)
    units_in = (unit_rows * norm_gain[1] + norm_bias[1]).astype(jnp.bfloat16)
    branch_grad = grad_rows * valid_rows
    branch_in = branch_grad.astype(jnp.bfloat16)

    near_unit, _ = unit(near_hidden)
    near_heads_in = (near_unit * norm_gain[0] + norm_bias[0]).astype(jnp.bfloat16)
    near_units_in = (near_unit * norm_gain[1] + norm_bias[1]).astype(jnp.bfloat16)
    near_branch_in = (near_grad * near_valid).astype(jnp.bfloat16)

    chosen = selection(model_width)

    def mine_theirs(rows):
        width = rows.shape[1] // 2
        low, high = rows[:, :width], rows[:, width:]
        return jnp.where(core == 0, low, high), jnp.where(core == 0, high, low)

    hidden_pre = jnp.dot(units_in, up_weight, preferred_element_type=jnp.float32) + up_bias
    activated_wide = gelu_exact(hidden_pre)
    activated = activated_wide.astype(jnp.bfloat16)
    mine, theirs = mine_theirs(activated_wide)
    near_activated = shift(theirs, CORE, 1)
    branch_left = pick(chosen, jnp.concatenate([branch_in, near_branch_in], axis=0))
    next_a, last_a, rest_a = products((branch_left, mine.astype(jnp.bfloat16), near_activated))
    minus_a, plus_a = ring(next_a, True, 1), ring(last_a, True, -1)

    pre_grad = jnp.dot(branch_in, down_weight, preferred_element_type=jnp.float32) * gelu_slope(
        hidden_pre
    )
    pre_in = pre_grad.astype(jnp.bfloat16)
    mine, theirs = mine_theirs(pre_grad)
    near_pre = shift(theirs, CORE, 1)
    units_left = pick(chosen, jnp.concatenate([units_in, near_units_in], axis=0))
    next_b, last_b, rest_b = products((units_left, mine.astype(jnp.bfloat16), near_pre))
    minus_b, plus_b = ring(next_b, True, 1), ring(last_b, True, -1)

    def middle(rest, minus, plus):
        half = rest.shape[0] // 4
        low = ring(rest[:half] + minus[half:], True, 1)
        high = ring(rest[half : 2 * half] + plus[:half], True, -1)
        return low, high

    def finish(rest, minus, plus, low, high):
        half = rest.shape[0] // 4
        return (
            rest[2 * half :]
            + jnp.concatenate([plus[half:], minus[:half]], axis=0)
            + jnp.concatenate([low, high], axis=0)
        )

    heads_in = tie(heads_in, next_b, last_b)
    projected = jnp.dot(heads_in, qkv_weight, preferred_element_type=jnp.float32)
    context_grad = jnp.dot(branch_in, dense_weight, preferred_element_type=jnp.float32)
    projected = tie(projected, minus_a, plus_a)
    low_a, high_a = middle(rest_a, minus_a, plus_a)
    context, projected_wide, projected_grad = attention(
        projected, context_grad, segment, cosine_table, sine_table
    )
    mine_c, theirs_c = mine_theirs(context.astype(jnp.float32))
    mine_q, theirs_q = mine_theirs(projected_wide)
    near_right = shift(jnp.concatenate([theirs_c, theirs_q], axis=1), CORE, 1)
    split = mine_c.shape[1]
    heads_left = pick(chosen, jnp.concatenate([heads_in, near_heads_in], axis=0))
    next_c, last_c, rest_c = products(
        (branch_left, mine_c.astype(jnp.bfloat16), near_right[:, :split]),
        (heads_left, mine_q.astype(jnp.bfloat16), near_right[:, split:]),
    )
    low_b, high_b = middle(rest_b, minus_b, plus_b)
    minus_c, plus_c = ring(next_c, True, 1), ring(last_c, True, -1)

    activated = tie(activated, next_c, last_c, minus_b, plus_b)
    partial_rows = lax.dot_general(
        context, dense_weight, CONTRACT_COLS, preferred_element_type=jnp.float32
    ) + lax.dot_general(
        activated, down_weight, CONTRACT_COLS, preferred_element_type=jnp.float32
    )
    branch = partial_rows + shift(partial_rows, TENSOR, 1)
    output = hidden + valid_rows * (branch + down_bias)

    projected_grad = tie(projected_grad, next_c, last_c, low_a, high_a)
    heads_grad = lax.dot_general(
        projected_grad, qkv_weight, CONTRACT_COLS, preferred_element_type=jnp.float32
    )
    units_grad = lax.dot_general(
        pre_in, up_weight, CONTRACT_COLS, preferred_element_type=jnp.float32
    )
    local_back = normalize_back(
        heads_grad, unit_rows, inv_scale, norm_gain[0]
    ) + normalize_back(units_grad, unit_rows, inv_scale, norm_gain[1])

    small = jnp.concatenate(
        [
            jnp.sum(heads_grad * unit_rows, axis=0)[None],
            jnp.sum(units_grad * unit_rows, axis=0)[None],
            jnp.sum(heads_grad, axis=0)[None],
            jnp.sum(units_grad, axis=0)[None],
            jnp.sum(branch_grad, axis=0)[None],
            jnp.sum(pre_grad, axis=0).reshape(table_rows, model_width),
        ],
        axis=0,
    )
    small = jnp.pad(small, ((0, 8 - small.shape[0]), (0, 0)))
    near_back = shift(jnp.concatenate([local_back, small], axis=0), TENSOR, 1)
    input_grad = grad_rows + (local_back + near_back[:row_count])
    summed = jnp.arange(8)[:, None] < 4
    small = small + jnp.where(summed, near_back[row_count:], 0.0)
    minus, plus = ring(small, True, 1), ring(small, True, -1)
    small = small + (minus + plus) + ring(minus, True, 1)

    def second(rows, extra):
        quarter = rows.shape[0] // 4
        half = quarter // 2
        count = extra.shape[0]
        minus = ring(jnp.concatenate([rows[half : 3 * half], extra]), False, 1)
        plus = ring(jnp.concatenate([rows[3 * half : 5 * half], extra]), False, -1)
        low = ring(
            jnp.concatenate([rows[:half] + minus[half:quarter], minus[quarter:]]), False, 1
        )
        high = ring(rows[5 * half : 6 * half] + plus[:half], False, -1)
        rows = (
            rows[6 * half :]
            + jnp.concatenate([plus[half:quarter], minus[:half]], axis=0)
            + jnp.concatenate([low[:half], high], axis=0)
        )
        extra = extra + (minus[quarter:] + plus[quarter:]) + low[half:]
        other = shift(jnp.concatenate([rows[:half], extra]), ZH, 1)
        return rows[half:] + other[:half], extra + other[half:]

    none = jnp.zeros((0, 2 * model_width), jnp.float32)
    sum_a = finish(rest_a, minus_a, plus_a, low_a, high_a)
    sum_b = finish(rest_b, minus_b, plus_b, low_b, high_b)
    early, _ = second(jnp.concatenate([sum_a, sum_b], axis=1), none)
    low_c, high_c = middle(rest_c, minus_c, plus_c)
    sum_c = finish(rest_c, minus_c, plus_c, low_c, high_c)
    late, small = second(sum_c, small)

    keep = early.shape[0] // 2
    near_early = shift(early[:keep], CORE, 1)
    near_late = shift(jnp.concatenate([late[:keep], small]), CORE, 1)
    small = small + near_late[keep:]

    def joined(own, near):
        return jnp.concatenate(
            [jnp.where(core == 0, own, near), jnp.where(core == 0, near, own)], axis=1
        )

    column = hidden_cols // 2
    down_grad = joined(early[keep:, :column], near_early[:, :column])
    up_grad = joined(early[keep:, column:], near_early[:, column:])
    dense_grad = joined(late[keep:, :split], near_late[:keep, :split])
    qkv_grad = joined(late[keep:, split:], near_late[:keep, split:])
    block = model_width // lax.axis_size(DP)
    small = lax.dynamic_slice_in_dim(small, group * block, block, axis=1)
    return (
        output,
        input_grad,
        qkv_grad[None],
        dense_grad[None],
        up_grad[None],
        down_grad[None],
        small[5 : 5 + table_rows][None],
        small[4][None],
        small[:2][None],
        small[2:4][None],
    )


def solution(mesh):
    split = Mesh(
        mesh.devices.reshape(4, 4, 2, 2, mesh.shape["tensor"]),
        (*DP, TENSOR),
    )
    in_specs = (
        P(DP, None),
        P(DP, None),
        P(None, None, "tensor"),
        P(None, None, "tensor"),
        P(None, None, "tensor"),
        P(None, None, "tensor"),
        P(None, "tensor"),
        P(),
        P(),
        P(),
        P(),
        P(),
        P(),
    )
    out_specs = (
        P(DP, None),
        P(DP, None),
        P(None, DP, "tensor"),
        P(None, DP, "tensor"),
        P(None, DP, "tensor"),
        P(None, DP, "tensor"),
        P(None, "tensor", DP),
        P(None, DP),
        P(None, None, DP),
        P(None, None, DP),
    )
    return jax.shard_map(
        shards, mesh=split, in_specs=in_specs, out_specs=out_specs, check_vma=False
    )
```

```python
import functools

import jax
import jax.numpy as jnp
from jax import lax
from jax.experimental import pallas as pl
from jax.experimental.pallas import tpu as pltpu
from jax.sharding import Mesh
from jax.sharding import PartitionSpec as P

HEAD_DIM = 64
ROTARY = 16
DP = ("dp_0", "dp_1", "dp_2", "dp_3")
X, Y, ZH, CORE = DP
TENSOR = "tensor"

epsilon = 1e-05

CONTRACT_COLS = (((1,), (1,)), ((), ()))


def shift(array, axis, step):
    size = lax.axis_size(axis)
    return lax.ppermute(array, axis, [(i, (i + step) % size) for i in range(size)])


def layout_rows(lengths, owner_group, row_offset, row_index, group_rows):
    first_row = owner_group * group_rows + row_offset
    inside = (row_index[:, None] >= first_row[None, :]) & (
        row_index[:, None] < (first_row + lengths)[None, :]
    )
    number = jnp.arange(lengths.shape[0], dtype=jnp.int32) + 1
    segment = jnp.sum(jnp.where(inside, number[None, :], 0), axis=1) - 1
    position = jnp.sum(jnp.where(inside, row_index[:, None] - first_row[None, :], 0), axis=1)
    return (segment, position)


def rotary_tables(position):
    lane = jnp.arange(2 * HEAD_DIM, dtype=jnp.int32) % HEAD_DIM
    half_rot = ROTARY // 2
    frequency = 1.0 / 10000.0 ** ((lane % half_rot).astype(jnp.float32) * 2.0 / ROTARY)
    angles = position.astype(jnp.float32)[:, None] * frequency[None, :]
    turned = (lane < ROTARY)[None, :]
    sign = jnp.where(lane < half_rot, -1.0, 1.0)[None, :]
    return (jnp.where(turned, jnp.cos(angles), 1.0), jnp.where(turned, jnp.sin(angles) * sign, 0.0))


def normalize_back(grad_rows, unit_rows, inv_scale, gain_row):
    scaled = grad_rows * gain_row
    return inv_scale * (
        scaled
        - jnp.mean(scaled, axis=-1, keepdims=True)
        - unit_rows * jnp.mean(scaled * unit_rows, axis=-1, keepdims=True)
    )


def attention_kernel(
    core,
    projected,
    context_grad,
    segment_column,
    segment_row,
    cosine,
    sine,
    context,
    grad,
    mine,
    theirs,
    turned,
    raw,
):
    rows, cols = projected.shape
    heads = cols // (3 * HEAD_DIM)
    lane = lax.broadcasted_iota(jnp.int32, (rows, 128), 1)
    entry = lane % HEAD_DIM
    scale = HEAD_DIM ** (-0.5)
    tables = []
    for kind in range(3):
        halves = [(2 * kind + side) % 3 for side in range(2)]
        cos_t, sin_t = cosine[...], sine[...]
        low = lane < HEAD_DIM
        for side, what in enumerate(halves):
            here = low if side == 0 else jnp.logical_not(low)
            if what == 0:
                cos_t = jnp.where(here, cos_t * scale, cos_t)
                sin_t = jnp.where(here, sin_t * scale, sin_t)
            if what == 2:
                cos_t = jnp.where(here, 1.0, cos_t)
                sin_t = jnp.where(here, 0.0, sin_t)
        tables.append((cos_t, sin_t))

    def swapped(part):
        up = pltpu.roll(part, 128 - ROTARY // 2, 1)
        down = pltpu.roll(part, ROTARY // 2, 1)
        return jnp.where(entry < ROTARY // 2, up, down)

    for chunk in range(cols // 128):
        at = slice(128 * chunk, 128 * (chunk + 1))
        part = projected[:, at]
        cos_t, sin_t = tables[chunk % 3]
        turned[:, at] = (part * cos_t + swapped(part) * sin_t).astype(jnp.bfloat16)

    allowed = (segment_column[...] == segment_row[...]) & (
        lax.broadcasted_iota(jnp.int32, (rows, rows), 1)
        <= lax.broadcasted_iota(jnp.int32, (rows, rows), 0)
    )

    def product(left, right, dims):
        return lax.dot_general(left, right, (dims, ((), ())), preferred_element_type=jnp.float32)

    for head in range(heads):
        base = 3 * HEAD_DIM * head
        query = turned[:, base : base + HEAD_DIM]
        key = turned[:, base + HEAD_DIM : base + 2 * HEAD_DIM]
        value = turned[:, base + 2 * HEAD_DIM : base + 3 * HEAD_DIM]
        at = slice(HEAD_DIM * head, HEAD_DIM * (head + 1))
        out_grad = context_grad[:, at].astype(jnp.bfloat16)
        scores = jnp.where(allowed, product(query, key, ((1,), (1,))), -1e30)
        highest = jnp.max(scores, axis=-1, keepdims=True)
        weights = jnp.where(allowed, jnp.exp(scores - highest), 0.0)
        probs = weights / jnp.sum(weights, axis=-1, keepdims=True)
        probs_low = probs.astype(jnp.bfloat16)
        out = product(probs_low, value, ((1,), (0,))).astype(jnp.bfloat16)
        context[:, at] = out
        offset = jnp.sum(
            out_grad.astype(jnp.float32) * out.astype(jnp.float32), axis=-1, keepdims=True
        )
        probs_grad = product(out_grad, value, ((1,), (1,)))
        score_grad = (probs * (probs_grad - offset)).astype(jnp.bfloat16)
        raw[:, base : base + HEAD_DIM] = product(score_grad, key, ((1,), (0,)))
        raw[:, base + HEAD_DIM : base + 2 * HEAD_DIM] = product(score_grad, query, ((0,), (0,)))
        raw[:, base + 2 * HEAD_DIM : base + 3 * HEAD_DIM] = product(
            probs_low, out_grad, ((0,), (0,))
        )

    for chunk in range(cols // 128):
        at = slice(128 * chunk, 128 * (chunk + 1))
        part = raw[:, at]
        cos_t, sin_t = tables[chunk % 3]
        back = part * cos_t - swapped(part) * sin_t
        raw[:, at] = back
        grad[:, at] = back.astype(jnp.bfloat16)

    for side in range(2):

        @pl.when(core[0] == side)
        def _():
            for out, half in ((mine, side), (theirs, 1 - side)):
                for whole, start in ((context, 0), (raw, context.shape[1] // 2)):
                    width = whole.shape[1] // 2
                    out[:, start : start + width] = whole[
                        :, half * width : (half + 1) * width
                    ].astype(out.dtype)


def attention(core, projected, context_grad, segment, cosine, sine):
    rows, cols = projected.shape
    width = (cols + context_grad.shape[1]) // 2
    vmem = pl.BlockSpec(memory_space=pltpu.VMEM)
    return pl.pallas_call(
        attention_kernel,
        in_specs=[pl.BlockSpec(memory_space=pltpu.SMEM)] + [vmem] * 6,
        out_shape=(
            jax.ShapeDtypeStruct(context_grad.shape, jnp.bfloat16),
            jax.ShapeDtypeStruct((rows, cols), jnp.bfloat16),
            jax.ShapeDtypeStruct((rows, width), jnp.bfloat16),
            jax.ShapeDtypeStruct((rows, width), jnp.float32),
        ),
        scratch_shapes=[
            pltpu.VMEM((rows, cols), jnp.bfloat16),
            pltpu.VMEM((rows, cols), jnp.float32),
        ],
        name="attention",
    )(core, projected, context_grad, segment[:, None], segment[None, :], cosine, sine)


def prologue_kernel(
    rows_in, grads_in, valid, gain, bias, message, branch_in, units_in, heads_in, unit_rows, inv_scale
):
    width = rows_in.shape[1]
    hidden = rows_in[...].astype(jnp.float32)
    centred = hidden - jnp.mean(hidden, axis=-1, keepdims=True)
    inv = lax.rsqrt(jnp.mean(centred * centred, axis=-1, keepdims=True) + epsilon)
    unit = centred * inv
    inv_scale[...] = inv
    unit_rows[...] = unit
    branch = grads_in[...].astype(jnp.float32) * valid[...]
    message[:, :width] = branch
    branch_in[...] = branch.astype(jnp.bfloat16)
    heads = unit * gain[0:1, :] + bias[0:1, :]
    units = unit * gain[1:2, :] + bias[1:2, :]
    message[:, width : 2 * width] = units
    units_in[...] = units.astype(jnp.bfloat16)
    message[:, 2 * width :] = heads
    heads_in[...] = heads.astype(jnp.bfloat16)


def prologue(rows_in, grads_in, valid, gain, bias):
    rows, width = rows_in.shape
    low = jax.ShapeDtypeStruct((rows, width), jnp.bfloat16)
    return pl.pallas_call(
        prologue_kernel,
        out_shape=(
            jax.ShapeDtypeStruct((rows, 3 * width), jnp.float32),
            low,
            low,
            low,
            jax.ShapeDtypeStruct((rows, width), jnp.float32),
            jax.ShapeDtypeStruct((rows, 1), jnp.float32),
        ),
        name="prologue",
    )(rows_in, grads_in, valid, gain, bias)


PIECES = 4


def order(step, core):
    return ((1 - core[0]) * (PIECES // 2) + step) % PIECES


def first_half(step, core):
    return (0, jnp.minimum(step, PIECES // 2 - 1))


def second_half(step, core):
    return (0, jnp.maximum(step - PIECES // 2, 0))


def up_kernel(core, units_in, weight, bias, activated, slope, mine, theirs):
    before = jnp.dot(units_in[...], weight[...], preferred_element_type=jnp.float32) + bias[...]
    rise = 0.5 * (1.0 + lax.erf(before * 0.7071067811865476))
    after = before * rise
    low = after.astype(jnp.bfloat16)
    activated[...] = low
    slope[...] = rise + before * jnp.exp(-0.5 * before * before) * 0.3989422804014327

    @pl.when(pl.program_id(0) < PIECES // 2)
    def _():
        theirs[...] = after

    @pl.when(pl.program_id(0) >= PIECES // 2)
    def _():
        mine[...] = low


def down_kernel(core, branch_in, weight, slope, pre_in, sums, mine, theirs):
    grad = jnp.dot(branch_in[...], weight[...], preferred_element_type=jnp.float32) * slope[...]
    low = grad.astype(jnp.bfloat16)
    pre_in[...] = low
    sums[...] = jnp.sum(grad, axis=0, keepdims=True)

    @pl.when(pl.program_id(0) < PIECES // 2)
    def _():
        theirs[...] = grad

    @pl.when(pl.program_id(0) >= PIECES // 2)
    def _():
        mine[...] = low


def hidden_call(kernel, name, core, rows_in, weight, extra, outs):
    rows, width = rows_in.shape
    cols = weight.shape[1]
    piece = cols // PIECES

    def whole(height):
        return pl.BlockSpec((height, piece), lambda step, core: (0, order(step, core)))

    return pl.pallas_call(
        kernel,
        grid_spec=pltpu.PrefetchScalarGridSpec(
            num_scalar_prefetch=1,
            grid=(PIECES,),
            in_specs=[
                pl.BlockSpec((rows, width), lambda step, core: (0, 0)),
                whole(width),
                whole(extra.shape[0]),
            ],
            out_specs=[whole(height) for height, _ in outs]
            + [pl.BlockSpec((rows, piece), second_half), pl.BlockSpec((rows, piece), first_half)],
        ),
        out_shape=[jax.ShapeDtypeStruct((height, cols), dtype) for height, dtype in outs]
        + [
            jax.ShapeDtypeStruct((rows, cols // 2), jnp.bfloat16),
            jax.ShapeDtypeStruct((rows, cols // 2), jnp.float32),
        ],
        name=name,
    )(core, rows_in, weight, extra)


def product_kernel(splits, *refs):
    lefts, (own, near) = refs[: len(splits)], refs[len(splits) : len(splits) + 2]
    low, high, kept, to_next, to_last = refs[len(splits) + 2 :]
    right = jnp.concatenate([own[...], near[...].astype(jnp.bfloat16)], axis=0)
    for left, (start, stop) in zip(lefts, splits):
        eighth = left.shape[0] // 8
        targets = (
            (low, 0), (to_next, 0), (to_next, 1), (to_last, 0), (to_last, 1), (high, 0), (kept, 0), (kept, 1),
        )
        for block, (out, place) in enumerate(targets):
            out[place * eighth : (place + 1) * eighth, start:stop] = jnp.dot(
                left[block * eighth : (block + 1) * eighth, :],
                right[:, start:stop],
                preferred_element_type=jnp.float32,
            )


def products(lefts, splits, own, near):
    rows, cols = lefts[0].shape[0], own.shape[1]
    sizes = (rows // 8, rows // 8, rows // 4, rows // 4, rows // 4)
    return pl.pallas_call(
        functools.partial(product_kernel, splits),
        out_shape=tuple(jax.ShapeDtypeStruct((size, cols), jnp.float32) for size in sizes),
        name="products",
    )(*lefts, own, near)


def middle_kernel(low, high, minus, plus, low_out, high_out):
    low_out[...] = low[...] + minus[...]
    high_out[...] = high[...] + plus[...]


def middle(low, high, minus, plus):
    half, cols = low.shape
    pieces = 4
    block = (half, cols // pieces)
    same = pl.BlockSpec(block, lambda i: (0, i))
    shape = jax.ShapeDtypeStruct(low.shape, jnp.float32)
    return pl.pallas_call(
        middle_kernel,
        grid=(pieces,),
        in_specs=[same, same, pl.BlockSpec(block, lambda i: (1, i)), same],
        out_specs=[same, same],
        out_shape=(shape, shape),
        name="middle",
    )(low, high, minus, plus)


def finish(kept, minus, plus, low, high):
    half = kept.shape[0] // 2
    return (
        kept
        + jnp.concatenate([plus[half:], minus[:half]], axis=0)
        + jnp.concatenate([low, high], axis=0)
    )


def moves():
    def along(first, step):
        pairs = []
        for index in range(64):
            x, y, rest, core = index // 16, index // 4 % 4, index % 4, index % 2
            if (core == 0) == first:
                x = (x + step) % 4
            else:
                y = (y + step) % 4
            pairs.append((index, x * 16 + y * 4 + rest))
        return pairs

    return {(first, step): along(first, step) for first in (True, False) for step in (1, -1)}


MOVES = moves()


def ring(array, first, step):
    return lax.ppermute(array, DP, MOVES[first, step])


def tie(values, *others):
    return lax.optimization_barrier((values, *others))[0]


def selection(width):
    ix, iy, iz, core = (lax.axis_index(axis) for axis in DP)
    row = jnp.arange(width, dtype=jnp.int32)
    block = width // 64
    inner = row % block
    at_core = core ^ (1 - row // block % 2)
    at_z = iz ^ (1 - row // (2 * block) % 2)
    second = row // (4 * block) % 4 + 1
    first = row // (16 * block) + 1
    at_x = (ix + jnp.where(core == 0, first, second)) % 4
    at_y = (iy + jnp.where(core == 0, second, first)) % 4
    feature = (((at_x * 4 + at_y) * 2 + at_z) * 2 + at_core) * block + inner
    column = jnp.arange(width, dtype=jnp.int32)
    return (feature[:, None] == column[None, :]).astype(jnp.bfloat16)


def pick_kernel(chosen, own, near, out):
    rows = jnp.concatenate([own[...], near[...].astype(jnp.bfloat16)], axis=0)
    out[...] = lax.dot_general(
        chosen[...], rows, CONTRACT_COLS, preferred_element_type=jnp.float32
    ).astype(jnp.bfloat16)


def pick(chosen, own, near, place):
    width = chosen.shape[0]
    rows = own.shape[0]
    pieces = 4
    return pl.pallas_call(
        pick_kernel,
        grid=(pieces,),
        in_specs=[
            pl.BlockSpec((width // pieces, width), lambda i: (i, 0)),
            pl.BlockSpec((rows, width), lambda i: (0, 0)),
            pl.BlockSpec((rows, width), lambda i: (0, place)),
        ],
        out_specs=pl.BlockSpec((width // pieces, 2 * rows), lambda i: (i, 0)),
        out_shape=jax.ShapeDtypeStruct((width, 2 * rows), jnp.bfloat16),
        name="pick",
    )(chosen, own, near)


def shards(
    block_input,
    cotangent,
    qkv_weight,
    dense_weight,
    up_weight,
    down_weight,
    up_bias,
    down_bias,
    norm_gain,
    norm_bias,
    lengths,
    owner_group,
    row_offset,
):
    row_count, model_width = block_input.shape
    qkv_weight, dense_weight = qkv_weight[0], dense_weight[0]
    up_weight, down_weight = up_weight[0], down_weight[0]
    norm_gain, norm_bias = norm_gain[0], norm_bias[0]
    hidden_cols = up_weight.shape[1]
    table_rows = hidden_cols // model_width

    group = lax.axis_index(DP)
    core = lax.axis_index(CORE)
    core_ref = core.astype(jnp.int32)[None]
    own_index = group * row_count + jnp.arange(row_count, dtype=jnp.int32)
    segment, position = layout_rows(lengths, owner_group, row_offset, own_index, row_count)
    valid_rows = (segment >= 0).astype(jnp.float32)[:, None]

    message, branch_in, units_in, heads_in, unit_rows, inv_scale = prologue(
        block_input, cotangent, valid_rows, norm_gain, norm_bias
    )
    near_rows = shift(message, CORE, 1)
    chosen = selection(model_width)

    def left_of(own, place):
        return pick(chosen, own, near_rows, place)

    activated, slope, mine_a, theirs_a = hidden_call(
        up_kernel,
        "up",
        core_ref,
        units_in,
        up_weight,
        up_bias,
        ((row_count, jnp.bfloat16), (row_count, jnp.float32)),
    )
    near_a = shift(theirs_a, CORE, 1)
    branch_left = left_of(tie(branch_in, theirs_a), 0)
    every = (0, mine_a.shape[1])
    low_a, high_a, kept_a, next_a, last_a = products((branch_left,), (every,), mine_a, near_a)
    minus_a, plus_a = ring(next_a, True, 1), ring(last_a, True, -1)

    pre_in, pre_sums, mine_b, theirs_b = hidden_call(
        down_kernel,
        "down",
        core_ref,
        tie(branch_in, next_a, last_a),
        down_weight,
        slope,
        ((row_count, jnp.bfloat16), (1, jnp.float32)),
    )
    near_b = shift(theirs_b, CORE, 1)
    units_left = left_of(tie(units_in, theirs_b), 1)
    low_b, high_b, kept_b, next_b, last_b = products((units_left,), (every,), mine_b, near_b)
    minus_b, plus_b = ring(next_b, True, 1), ring(last_b, True, -1)

    cosine_table, sine_table = rotary_tables(tie(position, next_b))
    heads_now, branch_now = tie((heads_in, branch_in), next_b, last_b)
    projected = jnp.dot(heads_now, qkv_weight, preferred_element_type=jnp.float32)
    context_grad = jnp.dot(branch_now, dense_weight, preferred_element_type=jnp.float32)
    low_a, high_a = middle(low_a, high_a, *tie((minus_a, plus_a), projected, context_grad))
    projected = tie(projected, low_a, high_a)
    low_a, high_a = ring(low_a, True, 1), ring(high_a, True, -1)
    context, projected_grad, mine_c, theirs_c = attention(
        core_ref, projected, context_grad, segment, cosine_table, sine_table
    )
    near_c = shift(theirs_c, CORE, 1)
    split = context.shape[1] // 2
    low_b, high_b = middle(low_b, high_b, *tie((minus_b, plus_b), theirs_c))
    heads_left = left_of(tie(heads_in, low_b, high_b), 2)
    low_b, high_b = ring(low_b, True, 1), ring(high_b, True, -1)
    low_c, high_c, kept_c, next_c, last_c = products(
        (branch_left, heads_left), ((0, split), (split, every[1])), mine_c, near_c
    )
    minus_c, plus_c = ring(next_c, True, 1), ring(last_c, True, -1)

    def second_send(rows, extra):
        half = rows.shape[0] // 8
        up = jnp.concatenate([rows[half : 3 * half], extra])
        down = jnp.concatenate([rows[3 * half : 5 * half], extra])
        return up, down

    def second_middle(rows, minus, plus):
        half = rows.shape[0] // 8
        low = jnp.concatenate([rows[:half] + minus[half : 2 * half], minus[2 * half :]])
        high = rows[5 * half : 6 * half] + plus[:half]
        return low, high

    def second_finish(rows, extra, minus, plus, low, high):
        half = rows.shape[0] // 8
        rows = (
            rows[6 * half :]
            + jnp.concatenate([plus[half : 2 * half], minus[:half]], axis=0)
            + jnp.concatenate([low[:half], high], axis=0)
        )
        return rows, extra + (minus[2 * half :] + plus[2 * half :]) + low[half:]

    low_a, high_a, low_b, high_b = tie((low_a, high_a, low_b, high_b), next_c, last_c)
    early = jnp.concatenate(
        [
            finish(kept_a, minus_a, plus_a, low_a, high_a),
            finish(kept_b, minus_b, plus_b, low_b, high_b),
        ],
        axis=1,
    )
    none = jnp.zeros((0, early.shape[1]), jnp.float32)
    up_early, down_early = second_send(early, none)
    projected_grad, pre_in = tie((projected_grad, pre_in), up_early, down_early)
    minus_e, plus_e = ring(up_early, False, 1), ring(down_early, False, -1)

    heads_grad = lax.dot_general(
        projected_grad, qkv_weight, CONTRACT_COLS, preferred_element_type=jnp.float32
    )
    units_grad = lax.dot_general(
        pre_in, up_weight, CONTRACT_COLS, preferred_element_type=jnp.float32
    )
    local_back = normalize_back(
        heads_grad, unit_rows, inv_scale, norm_gain[0]
    ) + normalize_back(units_grad, unit_rows, inv_scale, norm_gain[1])
    grad_rows = cotangent.astype(jnp.float32)

    small = jnp.concatenate(
        [
            jnp.sum(heads_grad * unit_rows, axis=0)[None],
            jnp.sum(units_grad * unit_rows, axis=0)[None],
            jnp.sum(heads_grad, axis=0)[None],
            jnp.sum(units_grad, axis=0)[None],
            jnp.sum(message[:, :model_width], axis=0)[None],
            pre_sums.reshape(table_rows, model_width),
        ],
        axis=0,
    )
    small = jnp.pad(small, ((0, 8 - small.shape[0]), (0, 0)))
    back_out = jnp.concatenate([local_back, small], axis=0)
    near_back = shift(back_out, TENSOR, 1)

    low_c, high_c = middle(low_c, high_c, *tie((minus_c, plus_c), back_out))
    activated = tie(activated, low_c, high_c)
    low_c, high_c = ring(low_c, True, 1), ring(high_c, True, -1)
    minus_e, plus_e = tie((minus_e, plus_e), activated)
    low_e, high_e = second_middle(early, minus_e, plus_e)
    activated = tie(activated, low_e, high_e)
    low_e, high_e = ring(low_e, False, 1), ring(high_e, False, -1)
    partial_rows = lax.dot_general(
        context, dense_weight, CONTRACT_COLS, preferred_element_type=jnp.float32
    ) + lax.dot_general(
        activated, down_weight, CONTRACT_COLS, preferred_element_type=jnp.float32
    )
    near_back = tie(near_back, partial_rows)
    near_partial = shift(partial_rows, TENSOR, 1)

    summed = jnp.arange(8)[:, None] < 4
    small = small + jnp.where(summed, near_back[row_count:], 0.0)
    small_minus, small_plus = ring(small, True, 1), ring(small, True, -1)
    low_c, high_c = tie((low_c, high_c), small)
    late = finish(kept_c, minus_c, plus_c, low_c, high_c)
    small = small + (small_minus + small_plus) + ring(small_minus, True, 1)
    up_late, down_late = second_send(late, small)
    minus_l, plus_l = ring(up_late, False, 1), ring(down_late, False, -1)

    low_e, high_e, near_partial, near_back = tie(
        (low_e, high_e, near_partial, near_back), up_late, down_late
    )
    early, _ = second_finish(early, none, minus_e, plus_e, low_e, high_e)
    keep = early.shape[0] // 2
    other_early = shift(early[:keep], ZH, 1)
    input_grad = grad_rows + (local_back + near_back[:row_count])
    minus_l, plus_l = tie((minus_l, plus_l), early)
    low_l, high_l = second_middle(late, minus_l, plus_l)
    near_partial = tie(near_partial, low_l, high_l)
    low_l, high_l = ring(low_l, False, 1), ring(high_l, False, -1)
    output = block_input.astype(jnp.float32) + valid_rows * (
        (partial_rows + near_partial) + down_bias
    )
    early = early[keep:] + other_early
    half = keep // 2
    near_early = shift(early[:half], CORE, 1)
    late, small = second_finish(late, small, minus_l, plus_l, low_l, high_l)
    other_late = shift(jnp.concatenate([late[:keep], small]), ZH, 1)
    late = late[keep:] + other_late[:keep]
    small = small + other_late[keep:]
    near_late = shift(jnp.concatenate([late[:half], small]), CORE, 1)
    small = small + near_late[half:]

    def joined(own, near):
        return jnp.concatenate(
            [jnp.where(core == 0, own, near), jnp.where(core == 0, near, own)], axis=1
        )

    column = hidden_cols // 2
    down_grad = joined(early[half:, :column], near_early[:, :column])
    up_grad = joined(early[half:, column:], near_early[:, column:])
    dense_grad = joined(late[half:, :split], near_late[:half, :split])
    qkv_grad = joined(late[half:, split:], near_late[:half, split:])
    block = model_width // lax.axis_size(DP)
    small = lax.dynamic_slice_in_dim(small, group * block, block, axis=1)
    return (
        output,
        input_grad,
        qkv_grad[None],
        dense_grad[None],
        up_grad[None],
        down_grad[None],
        small[5 : 5 + table_rows][None],
        small[4][None],
        small[:2][None],
        small[2:4][None],
    )


def solution(mesh):
    split = Mesh(
        mesh.devices.reshape(4, 4, 2, 2, mesh.shape["tensor"]),
        (*DP, TENSOR),
    )
    in_specs = (
        P(DP, None),
        P(DP, None),
        P(None, None, "tensor"),
        P(None, None, "tensor"),
        P(None, None, "tensor"),
        P(None, None, "tensor"),
        P(None, "tensor"),
        P(),
        P(),
        P(),
        P(),
        P(),
        P(),
    )
    out_specs = (
        P(DP, None),
        P(DP, None),
        P(None, DP, "tensor"),
        P(None, DP, "tensor"),
        P(None, DP, "tensor"),
        P(None, DP, "tensor"),
        P(None, "tensor", DP),
        P(None, DP),
        P(None, None, DP),
        P(None, None, DP),
    )
    return jax.shard_map(
        shards, mesh=split, in_specs=in_specs, out_specs=out_specs, check_vma=False
    )
```

```python
import functools

import jax
import jax.numpy as jnp
from jax import lax
from jax.experimental import pallas as pl
from jax.experimental.pallas import tpu as pltpu
from jax.sharding import Mesh
from jax.sharding import PartitionSpec as P

HEAD_DIM = 64
ROTARY = 16
DP = ("dp_0", "dp_1", "dp_2", "dp_3")
X, Y, ZH, CORE = DP
TENSOR = "tensor"

epsilon = 1e-05

CONTRACT_COLS = (((1,), (1,)), ((), ()))


def shift(array, axis, step):
    size = lax.axis_size(axis)
    return lax.ppermute(array, axis, [(i, (i + step) % size) for i in range(size)])


def layout_rows(lengths, owner_group, row_offset, row_index, group_rows):
    first_row = owner_group * group_rows + row_offset
    inside = (row_index[:, None] >= first_row[None, :]) & (
        row_index[:, None] < (first_row + lengths)[None, :]
    )
    number = jnp.arange(lengths.shape[0], dtype=jnp.int32) + 1
    segment = jnp.sum(jnp.where(inside, number[None, :], 0), axis=1) - 1
    position = jnp.sum(jnp.where(inside, row_index[:, None] - first_row[None, :], 0), axis=1)
    return (segment, position)


def rotary_tables(position):
    lane = jnp.arange(2 * HEAD_DIM, dtype=jnp.int32) % HEAD_DIM
    half_rot = ROTARY // 2
    frequency = 1.0 / 10000.0 ** ((lane % half_rot).astype(jnp.float32) * 2.0 / ROTARY)
    angles = position.astype(jnp.float32)[:, None] * frequency[None, :]
    turned = (lane < ROTARY)[None, :]
    sign = jnp.where(lane < half_rot, -1.0, 1.0)[None, :]
    return (jnp.where(turned, jnp.cos(angles), 1.0), jnp.where(turned, jnp.sin(angles) * sign, 0.0))


def normalize_back(grad_rows, unit_rows, inv_scale, gain_row):
    scaled = grad_rows * gain_row
    return inv_scale * (
        scaled
        - jnp.mean(scaled, axis=-1, keepdims=True)
        - unit_rows * jnp.mean(scaled * unit_rows, axis=-1, keepdims=True)
    )


def attention_kernel(
    core,
    projected,
    context_grad,
    segment_column,
    segment_row,
    cosine,
    sine,
    context,
    grad,
    mine,
    theirs,
    turned,
    raw,
):
    rows, cols = projected.shape
    heads = cols // (3 * HEAD_DIM)
    lane = lax.broadcasted_iota(jnp.int32, (rows, 128), 1)
    entry = lane % HEAD_DIM
    scale = HEAD_DIM ** (-0.5)
    tables = []
    for kind in range(3):
        halves = [(2 * kind + side) % 3 for side in range(2)]
        cos_t, sin_t = cosine[...], sine[...]
        low = lane < HEAD_DIM
        for side, what in enumerate(halves):
            here = low if side == 0 else jnp.logical_not(low)
            if what == 0:
                cos_t = jnp.where(here, cos_t * scale, cos_t)
                sin_t = jnp.where(here, sin_t * scale, sin_t)
            if what == 2:
                cos_t = jnp.where(here, 1.0, cos_t)
                sin_t = jnp.where(here, 0.0, sin_t)
        tables.append((cos_t, sin_t))

    def swapped(part):
        up = pltpu.roll(part, 128 - ROTARY // 2, 1)
        down = pltpu.roll(part, ROTARY // 2, 1)
        return jnp.where(entry < ROTARY // 2, up, down)

    for chunk in range(cols // 128):
        at = slice(128 * chunk, 128 * (chunk + 1))
        part = projected[:, at]
        cos_t, sin_t = tables[chunk % 3]
        turned[:, at] = (part * cos_t + swapped(part) * sin_t).astype(jnp.bfloat16)

    allowed = (segment_column[...] == segment_row[...]) & (
        lax.broadcasted_iota(jnp.int32, (rows, rows), 1)
        <= lax.broadcasted_iota(jnp.int32, (rows, rows), 0)
    )

    def product(left, right, dims):
        return lax.dot_general(left, right, (dims, ((), ())), preferred_element_type=jnp.float32)

    for head in range(heads):
        base = 3 * HEAD_DIM * head
        query = turned[:, base : base + HEAD_DIM]
        key = turned[:, base + HEAD_DIM : base + 2 * HEAD_DIM]
        value = turned[:, base + 2 * HEAD_DIM : base + 3 * HEAD_DIM]
        at = slice(HEAD_DIM * head, HEAD_DIM * (head + 1))
        out_grad = context_grad[:, at].astype(jnp.bfloat16)
        scores = jnp.where(allowed, product(query, key, ((1,), (1,))), -1e30)
        highest = jnp.max(scores, axis=-1, keepdims=True)
        weights = jnp.where(allowed, jnp.exp(scores - highest), 0.0)
        probs = weights / jnp.sum(weights, axis=-1, keepdims=True)
        probs_low = probs.astype(jnp.bfloat16)
        out = product(probs_low, value, ((1,), (0,))).astype(jnp.bfloat16)
        context[:, at] = out
        offset = jnp.sum(
            out_grad.astype(jnp.float32) * out.astype(jnp.float32), axis=-1, keepdims=True
        )
        probs_grad = product(out_grad, value, ((1,), (1,)))
        score_grad = (probs * (probs_grad - offset)).astype(jnp.bfloat16)
        raw[:, base : base + HEAD_DIM] = product(score_grad, key, ((1,), (0,)))
        raw[:, base + HEAD_DIM : base + 2 * HEAD_DIM] = product(score_grad, query, ((0,), (0,)))
        raw[:, base + 2 * HEAD_DIM : base + 3 * HEAD_DIM] = product(
            probs_low, out_grad, ((0,), (0,))
        )

    for chunk in range(cols // 128):
        at = slice(128 * chunk, 128 * (chunk + 1))
        part = raw[:, at]
        cos_t, sin_t = tables[chunk % 3]
        back = part * cos_t - swapped(part) * sin_t
        raw[:, at] = back
        grad[:, at] = back.astype(jnp.bfloat16)

    for side in range(2):

        @pl.when(core[0] == side)
        def _():
            for out, half in ((mine, side), (theirs, 1 - side)):
                for whole, start in ((context, 0), (raw, context.shape[1] // 2)):
                    width = whole.shape[1] // 2
                    out[:, start : start + width] = whole[
                        :, half * width : (half + 1) * width
                    ].astype(out.dtype)


def attention(core, projected, context_grad, segment, cosine, sine):
    rows, cols = projected.shape
    width = (cols + context_grad.shape[1]) // 2
    vmem = pl.BlockSpec(memory_space=pltpu.VMEM)
    return pl.pallas_call(
        attention_kernel,
        in_specs=[pl.BlockSpec(memory_space=pltpu.SMEM)] + [vmem] * 6,
        out_shape=(
            jax.ShapeDtypeStruct(context_grad.shape, jnp.bfloat16),
            jax.ShapeDtypeStruct((rows, cols), jnp.bfloat16),
            jax.ShapeDtypeStruct((rows, width), jnp.bfloat16),
            jax.ShapeDtypeStruct((rows, width), jnp.float32),
        ),
        scratch_shapes=[
            pltpu.VMEM((rows, cols), jnp.bfloat16),
            pltpu.VMEM((rows, cols), jnp.float32),
        ],
        name="attention",
    )(core, projected, context_grad, segment[:, None], segment[None, :], cosine, sine)


def prologue_kernel(
    rows_in, grads_in, valid, gain, bias, message, branch_in, units_in, heads_in, unit_rows, inv_scale, sums
):
    width = rows_in.shape[1]
    hidden = rows_in[...].astype(jnp.float32)
    centred = hidden - jnp.mean(hidden, axis=-1, keepdims=True)
    inv = lax.rsqrt(jnp.mean(centred * centred, axis=-1, keepdims=True) + epsilon)
    unit = centred * inv
    inv_scale[...] = inv
    unit_rows[...] = unit
    branch = grads_in[...].astype(jnp.float32) * valid[...]
    message[:, :width] = branch
    sums[...] = jnp.sum(branch, axis=0, keepdims=True)
    branch_in[...] = branch.astype(jnp.bfloat16)
    heads = unit * gain[0:1, :] + bias[0:1, :]
    units = unit * gain[1:2, :] + bias[1:2, :]
    message[:, width : 2 * width] = units
    units_in[...] = units.astype(jnp.bfloat16)
    message[:, 2 * width :] = heads
    heads_in[...] = heads.astype(jnp.bfloat16)


def prologue(rows_in, grads_in, valid, gain, bias):
    rows, width = rows_in.shape
    low = jax.ShapeDtypeStruct((rows, width), jnp.bfloat16)
    return pl.pallas_call(
        prologue_kernel,
        out_shape=(
            jax.ShapeDtypeStruct((rows, 3 * width), jnp.float32),
            low,
            low,
            low,
            jax.ShapeDtypeStruct((rows, width), jnp.float32),
            jax.ShapeDtypeStruct((rows, 1), jnp.float32),
            jax.ShapeDtypeStruct((1, width), jnp.float32),
        ),
        name="prologue",
    )(rows_in, grads_in, valid, gain, bias)


PIECES = 4


def order(step, core):
    return ((1 - core[0]) * (PIECES // 2) + step) % PIECES


def first_half(step, core):
    return (0, jnp.minimum(step, PIECES // 2 - 1))


def second_half(step, core):
    return (0, jnp.maximum(step - PIECES // 2, 0))


def up_kernel(core, units_in, weight, bias, activated, slope, mine, theirs):
    before = jnp.dot(units_in[...], weight[...], preferred_element_type=jnp.float32) + bias[...]
    rise = 0.5 * (1.0 + lax.erf(before * 0.7071067811865476))
    after = before * rise
    low = after.astype(jnp.bfloat16)
    activated[...] = low
    slope[...] = rise + before * jnp.exp(-0.5 * before * before) * 0.3989422804014327

    @pl.when(pl.program_id(0) < PIECES // 2)
    def _():
        theirs[...] = after

    @pl.when(pl.program_id(0) >= PIECES // 2)
    def _():
        mine[...] = low


def down_kernel(core, branch_in, weight, slope, pre_in, sums, mine, theirs):
    grad = jnp.dot(branch_in[...], weight[...], preferred_element_type=jnp.float32) * slope[...]
    low = grad.astype(jnp.bfloat16)
    pre_in[...] = low
    sums[...] = jnp.sum(grad, axis=0, keepdims=True)

    @pl.when(pl.program_id(0) < PIECES // 2)
    def _():
        theirs[...] = grad

    @pl.when(pl.program_id(0) >= PIECES // 2)
    def _():
        mine[...] = low


def hidden_call(kernel, name, core, rows_in, weight, extra, outs):
    rows, width = rows_in.shape
    cols = weight.shape[1]
    piece = cols // PIECES

    def whole(height):
        return pl.BlockSpec((height, piece), lambda step, core: (0, order(step, core)))

    return pl.pallas_call(
        kernel,
        grid_spec=pltpu.PrefetchScalarGridSpec(
            num_scalar_prefetch=1,
            grid=(PIECES,),
            in_specs=[
                pl.BlockSpec((rows, width), lambda step, core: (0, 0)),
                whole(width),
                whole(extra.shape[0]),
            ],
            out_specs=[whole(height) for height, _ in outs]
            + [pl.BlockSpec((rows, piece), second_half), pl.BlockSpec((rows, piece), first_half)],
        ),
        out_shape=[jax.ShapeDtypeStruct((height, cols), dtype) for height, dtype in outs]
        + [
            jax.ShapeDtypeStruct((rows, cols // 2), jnp.bfloat16),
            jax.ShapeDtypeStruct((rows, cols // 2), jnp.float32),
        ],
        name=name,
    )(core, rows_in, weight, extra)


def product_kernel(splits, *refs):
    lefts, (own, near) = refs[: len(splits)], refs[len(splits) : len(splits) + 2]
    low, high, kept, to_next, to_last = refs[len(splits) + 2 :]
    right = jnp.concatenate([own[...], near[...].astype(jnp.bfloat16)], axis=0)
    for left, (start, stop) in zip(lefts, splits):
        eighth = left.shape[0] // 8
        targets = (
            (low, 0), (to_next, 0), (to_next, 1), (to_last, 0), (to_last, 1), (high, 0), (kept, 0), (kept, 1),
        )
        for block, (out, place) in enumerate(targets):
            out[place * eighth : (place + 1) * eighth, start:stop] = jnp.dot(
                left[block * eighth : (block + 1) * eighth, :],
                right[:, start:stop],
                preferred_element_type=jnp.float32,
            )


def products(lefts, splits, own, near):
    rows, cols = lefts[0].shape[0], own.shape[1]
    sizes = (rows // 8, rows // 8, rows // 4, rows // 4, rows // 4)
    return pl.pallas_call(
        functools.partial(product_kernel, splits),
        out_shape=tuple(jax.ShapeDtypeStruct((size, cols), jnp.float32) for size in sizes),
        name="products",
    )(*lefts, own, near)


def middle(low, high, minus, plus):
    half = low.shape[0]
    return low + minus[half:], high + plus[:half]


def finish(kept, minus, plus, low, high):
    half = kept.shape[0] // 2
    first = kept[:half] + plus[half:] + low
    last = kept[half:] + minus[:half] + high
    return jnp.concatenate(lax.optimization_barrier((first, last)), axis=0)


def moves():
    def along(first, step):
        pairs = []
        for index in range(64):
            x, y, rest, core = index // 16, index // 4 % 4, index % 4, index % 2
            if (core == 0) == first:
                x = (x + step) % 4
            else:
                y = (y + step) % 4
            pairs.append((index, x * 16 + y * 4 + rest))
        return pairs

    return {(first, step): along(first, step) for first in (True, False) for step in (1, -1)}


MOVES = moves()


def ring(array, first, step):
    return lax.ppermute(array, DP, MOVES[first, step])


def tie(values, *others):
    return lax.optimization_barrier((values, *others))[0]


def selection(width):
    ix, iy, iz, core = (lax.axis_index(axis) for axis in DP)
    row = jnp.arange(width, dtype=jnp.int32)
    block = width // 64
    inner = row % block
    at_core = core ^ (1 - row // block % 2)
    at_z = iz ^ (1 - row // (2 * block) % 2)
    second = row // (4 * block) % 4 + 1
    first = row // (16 * block) + 1
    at_x = (ix + jnp.where(core == 0, first, second)) % 4
    at_y = (iy + jnp.where(core == 0, second, first)) % 4
    feature = (((at_x * 4 + at_y) * 2 + at_z) * 2 + at_core) * block + inner
    column = jnp.arange(width, dtype=jnp.int32)
    return (feature[:, None] == column[None, :]).astype(jnp.bfloat16)


def pick_kernel(chosen, own, near, out):
    rows = jnp.concatenate([own[...], near[...].astype(jnp.bfloat16)], axis=0)
    out[...] = lax.dot_general(
        chosen[...], rows, CONTRACT_COLS, preferred_element_type=jnp.float32
    ).astype(jnp.bfloat16)


def pick(chosen, own, near, place):
    width = chosen.shape[0]
    rows = own.shape[0]
    pieces = 4
    return pl.pallas_call(
        pick_kernel,
        grid=(pieces,),
        in_specs=[
            pl.BlockSpec((width // pieces, width), lambda i: (i, 0)),
            pl.BlockSpec((rows, width), lambda i: (0, 0)),
            pl.BlockSpec((rows, width), lambda i: (0, place)),
        ],
        out_specs=pl.BlockSpec((width // pieces, 2 * rows), lambda i: (i, 0)),
        out_shape=jax.ShapeDtypeStruct((width, 2 * rows), jnp.bfloat16),
        name="pick",
    )(chosen, own, near)


def shards(
    block_input,
    cotangent,
    qkv_weight,
    dense_weight,
    up_weight,
    down_weight,
    up_bias,
    down_bias,
    norm_gain,
    norm_bias,
    lengths,
    owner_group,
    row_offset,
):
    row_count, model_width = block_input.shape
    qkv_weight, dense_weight = qkv_weight[0], dense_weight[0]
    up_weight, down_weight = up_weight[0], down_weight[0]
    norm_gain, norm_bias = norm_gain[0], norm_bias[0]
    hidden_cols = up_weight.shape[1]
    table_rows = hidden_cols // model_width

    group = lax.axis_index(DP)
    core = lax.axis_index(CORE)
    core_ref = core.astype(jnp.int32)[None]
    own_index = group * row_count + jnp.arange(row_count, dtype=jnp.int32)
    segment, position = layout_rows(lengths, owner_group, row_offset, own_index, row_count)
    valid_rows = (segment >= 0).astype(jnp.float32)[:, None]

    message, branch_in, units_in, heads_in, unit_rows, inv_scale, branch_sums = prologue(
        block_input, cotangent, valid_rows, norm_gain, norm_bias
    )
    near_rows = shift(message, CORE, 1)
    chosen = selection(model_width)

    def left_of(own, place):
        return pick(chosen, own, near_rows, place)

    activated, slope, mine_a, theirs_a = hidden_call(
        up_kernel,
        "up",
        core_ref,
        units_in,
        up_weight,
        up_bias,
        ((row_count, jnp.bfloat16), (row_count, jnp.float32)),
    )
    near_a = shift(theirs_a, CORE, 1)
    branch_left = left_of(tie(branch_in, theirs_a), 0)
    every = (0, mine_a.shape[1])
    low_a, high_a, kept_a, next_a, last_a = products((branch_left,), (every,), mine_a, near_a)
    minus_a, plus_a = ring(next_a, True, 1), ring(last_a, True, -1)

    pre_in, pre_sums, mine_b, theirs_b = hidden_call(
        down_kernel,
        "down",
        core_ref,
        tie(branch_in, next_a, last_a),
        down_weight,
        slope,
        ((row_count, jnp.bfloat16), (1, jnp.float32)),
    )
    near_b = shift(theirs_b, CORE, 1)
    units_left = left_of(tie(units_in, theirs_b), 1)
    low_b, high_b, kept_b, next_b, last_b = products((units_left,), (every,), mine_b, near_b)
    minus_b, plus_b = ring(next_b, True, 1), ring(last_b, True, -1)

    cosine_table, sine_table = rotary_tables(tie(position, next_b))
    heads_now, branch_now = tie((heads_in, branch_in), next_b, last_b)
    projected = jnp.dot(heads_now, qkv_weight, preferred_element_type=jnp.float32)
    context_grad = jnp.dot(branch_now, dense_weight, preferred_element_type=jnp.float32)
    low_a, high_a = middle(low_a, high_a, *tie((minus_a, plus_a), projected, context_grad))
    projected = tie(projected, low_a, high_a)
    low_a, high_a = ring(low_a, True, 1), ring(high_a, True, -1)
    context, projected_grad, mine_c, theirs_c = attention(
        core_ref, projected, context_grad, segment, cosine_table, sine_table
    )
    near_c = shift(theirs_c, CORE, 1)
    split = context.shape[1] // 2
    low_b, high_b = middle(low_b, high_b, *tie((minus_b, plus_b), theirs_c))
    heads_left = left_of(tie(heads_in, low_b, high_b), 2)
    low_b, high_b = ring(low_b, True, 1), ring(high_b, True, -1)
    low_c, high_c, kept_c, next_c, last_c = products(
        (branch_left, heads_left), ((0, split), (split, every[1])), mine_c, near_c
    )
    minus_c, plus_c = ring(next_c, True, 1), ring(last_c, True, -1)

    def second_send(rows, extra):
        half = rows.shape[0] // 8
        up = jnp.concatenate([rows[half : 3 * half], extra])
        down = jnp.concatenate([rows[3 * half : 5 * half], extra])
        return up, down

    def second_middle(rows, minus, plus):
        half = rows.shape[0] // 8
        low = jnp.concatenate([rows[:half] + minus[half : 2 * half], minus[2 * half :]])
        high = rows[5 * half : 6 * half] + plus[:half]
        return low, high

    def second_finish(rows, extra, minus, plus, low, high):
        half = rows.shape[0] // 8
        rows = (
            rows[6 * half :]
            + jnp.concatenate([plus[half : 2 * half], minus[:half]], axis=0)
            + jnp.concatenate([low[:half], high], axis=0)
        )
        return rows, extra + (minus[2 * half :] + plus[2 * half :]) + low[half:]

    low_a, high_a, low_b, high_b = tie((low_a, high_a, low_b, high_b), next_c, last_c)
    early = jnp.concatenate(
        [
            finish(kept_a, minus_a, plus_a, low_a, high_a),
            finish(kept_b, minus_b, plus_b, low_b, high_b),
        ],
        axis=1,
    )
    none = jnp.zeros((0, early.shape[1]), jnp.float32)
    up_early, down_early = second_send(early, none)
    projected_grad, pre_in = tie((projected_grad, pre_in), up_early, down_early)
    minus_e, plus_e = ring(up_early, False, 1), ring(down_early, False, -1)

    heads_grad = lax.dot_general(
        projected_grad, qkv_weight, CONTRACT_COLS, preferred_element_type=jnp.float32
    )
    units_grad = lax.dot_general(
        pre_in, up_weight, CONTRACT_COLS, preferred_element_type=jnp.float32
    )
    local_back = normalize_back(
        heads_grad, unit_rows, inv_scale, norm_gain[0]
    ) + normalize_back(units_grad, unit_rows, inv_scale, norm_gain[1])
    grad_rows = cotangent.astype(jnp.float32)

    small = jnp.concatenate(
        [
            jnp.sum(heads_grad * unit_rows, axis=0)[None],
            jnp.sum(units_grad * unit_rows, axis=0)[None],
            jnp.sum(heads_grad, axis=0)[None],
            jnp.sum(units_grad, axis=0)[None],
            branch_sums,
            pre_sums.reshape(table_rows, model_width),
        ],
        axis=0,
    )
    small = jnp.pad(small, ((0, 8 - small.shape[0]), (0, 0)))
    back_out = jnp.concatenate([local_back, small], axis=0)
    near_back = shift(back_out, TENSOR, 1)

    low_c, high_c = middle(low_c, high_c, *tie((minus_c, plus_c), back_out))
    activated = tie(activated, low_c, high_c)
    low_c, high_c = ring(low_c, True, 1), ring(high_c, True, -1)
    minus_e, plus_e = tie((minus_e, plus_e), activated)
    low_e, high_e = second_middle(early, minus_e, plus_e)
    activated = tie(activated, low_e, high_e)
    low_e, high_e = ring(low_e, False, 1), ring(high_e, False, -1)
    partial_rows = lax.dot_general(
        context, dense_weight, CONTRACT_COLS, preferred_element_type=jnp.float32
    ) + lax.dot_general(
        activated, down_weight, CONTRACT_COLS, preferred_element_type=jnp.float32
    )
    near_back = tie(near_back, partial_rows)
    near_partial = shift(partial_rows, TENSOR, 1)

    summed = jnp.arange(8)[:, None] < 4
    small = small + jnp.where(summed, near_back[row_count:], 0.0)
    small_minus, small_plus = ring(small, True, 1), ring(small, True, -1)
    low_c, high_c = tie((low_c, high_c), small)
    late = finish(kept_c, minus_c, plus_c, low_c, high_c)
    small = small + (small_minus + small_plus) + ring(small_minus, True, 1)
    up_late, down_late = second_send(late, small)
    minus_l, plus_l = ring(up_late, False, 1), ring(down_late, False, -1)

    low_e, high_e, near_partial, near_back = tie(
        (low_e, high_e, near_partial, near_back), up_late, down_late
    )
    early, _ = second_finish(early, none, minus_e, plus_e, low_e, high_e)
    keep = early.shape[0] // 2
    other_early = shift(early[:keep], ZH, 1)
    input_grad = grad_rows + (local_back + near_back[:row_count])
    minus_l, plus_l = tie((minus_l, plus_l), early)
    low_l, high_l = second_middle(late, minus_l, plus_l)
    near_partial = tie(near_partial, low_l, high_l)
    low_l, high_l = ring(low_l, False, 1), ring(high_l, False, -1)
    output = block_input.astype(jnp.float32) + valid_rows * (
        (partial_rows + near_partial) + down_bias
    )
    early = early[keep:] + other_early
    half = keep // 2
    near_early = shift(early[:half], CORE, 1)
    late, small = second_finish(late, small, minus_l, plus_l, low_l, high_l)
    other_late = shift(jnp.concatenate([late[:keep], small]), ZH, 1)
    late = late[keep:] + other_late[:keep]
    small = small + other_late[keep:]
    near_late = shift(jnp.concatenate([late[:half], small]), CORE, 1)
    small = small + near_late[half:]

    def joined(own, near):
        return jnp.concatenate(
            [jnp.where(core == 0, own, near), jnp.where(core == 0, near, own)], axis=1
        )

    column = hidden_cols // 2
    down_grad = joined(early[half:, :column], near_early[:, :column])
    up_grad = joined(early[half:, column:], near_early[:, column:])
    dense_grad = joined(late[half:, :split], near_late[:half, :split])
    qkv_grad = joined(late[half:, split:], near_late[:half, split:])
    block = model_width // lax.axis_size(DP)
    small = lax.dynamic_slice_in_dim(small, group * block, block, axis=1)
    return (
        output,
        input_grad,
        qkv_grad[None],
        dense_grad[None],
        up_grad[None],
        down_grad[None],
        small[5 : 5 + table_rows][None],
        small[4][None],
        small[:2][None],
        small[2:4][None],
    )


def solution(mesh):
    split = Mesh(
        mesh.devices.reshape(4, 4, 2, 2, mesh.shape["tensor"]),
        (*DP, TENSOR),
    )
    in_specs = (
        P(DP, None),
        P(DP, None),
        P(None, None, "tensor"),
        P(None, None, "tensor"),
        P(None, None, "tensor"),
        P(None, None, "tensor"),
        P(None, "tensor"),
        P(),
        P(),
        P(),
        P(),
        P(),
        P(),
    )
    out_specs = (
        P(DP, None),
        P(DP, None),
        P(None, DP, "tensor"),
        P(None, DP, "tensor"),
        P(None, DP, "tensor"),
        P(None, DP, "tensor"),
        P(None, "tensor", DP),
        P(None, DP),
        P(None, None, DP),
        P(None, None, DP),
    )
    return jax.shard_map(
        shards, mesh=split, in_specs=in_specs, out_specs=out_specs, check_vma=False
    )
```
